32 devices in a mesh: dp: 8 (over z, core), tensor: 4 (over y, x).
Axes of the slice: x: 2, y: 2, z: 4, core: 2. Of those that a mesh axis runs over, the one named last changes fastest.
Arguments:
- layer_input: bfloat16 [8192, 2048], P(('dp', 'tensor')), may hold values from -6 to 6
- norm1_gain: bfloat16 [2048], P('dp'), may hold values from 0.25 to 1.75
- norm1_bias: bfloat16 [2048], P('dp'), may hold values from -3 to 3
- qkv_weight: bfloat16 [3, 2048, 2048], P(None, 'dp', 'tensor'), may hold values from -0.125 to 0.125
- qkv_bias: bfloat16 [3, 2048], P(None, ('tensor', 'dp')), may hold values from -6 to 6
- out_weight: bfloat16 [2048, 2048], P('tensor', 'dp'), may hold values from -0.5 to 0.5
- norm2_gain: bfloat16 [2048], P('dp'), may hold values from 0.25 to 1.75
- norm2_bias: bfloat16 [2048], P('dp'), may hold values from -3 to 3
- gate_up_weight: bfloat16 [2, 2048, 5632], P(None, 'dp', 'tensor'), may hold values from -0.125 to 0.125
- down_weight: bfloat16 [5632, 2048], P('tensor', 'dp'), may hold values from -0.15625 to 0.15625
- out_cotangent: bfloat16 [8192, 2048], P(('dp', 'tensor')), may hold values from -6 to 6
Outputs:
- layer_output: bfloat16 [8192, 2048], P(('dp', 'tensor'))
- grad_input: float32 [8192, 2048], P(('dp', 'tensor'))
- grad_norm1_gain: float32 [2048], P('dp')
- grad_norm1_bias: float32 [2048], P('dp')
- grad_qkv_weight: float32 [3, 2048, 2048], P(None, 'dp', 'tensor')
- grad_qkv_bias: float32 [3, 2048], P(None, ('tensor', 'dp'))
- grad_out_weight: float32 [2048, 2048], P('tensor', 'dp')
- grad_norm2_gain: float32 [2048], P('dp')
- grad_norm2_bias: float32 [2048], P('dp')
- grad_gate_up_weight: float32 [2, 2048, 5632], P(None, 'dp', 'tensor')
- grad_down_weight: float32 [5632, 2048], P('tensor', 'dp')
The draws below stay inside these ranges and needn't reach their ends.
All inputs are finite; a program needn't handle non-finite values.
Results may differ from the reference program's by a relative error of at most 0.025.
The reference program's roundings to bfloat16 on the way count: a program that leaves them out, or rounds other values in their place, can miss the bound.
Values may be sent and summed in bfloat16 or wider, within the bound.
No kernel may reach another device: no remote copies, remote signals or barrier semaphores. Data moves between devices by JAX's collectives and lax.ppermute only.
A program may use at most 192 MiB of HBM per device.

```python
import jax
import jax.numpy as jnp
from jax import lax

D = 2048
HEADS = 32
FF = 5632
HEAD_DIM = 64
ROT = 16
SEQ_LEN = 512
SEQ_DEV = 2
TOKENS = 8192
N_DP = 8
N_TENSOR = 4


def draw_qkv_bias(key, part):
    normal_base = jnp.clip(jax.random.normal(jax.random.fold_in(key, 11), (3, D), jnp.float32), -3.0, 3.0)
    return (0.5 * normal_base).astype(jnp.bfloat16)


def steps_of(rng, extent, cuts, smallest, largest):
    gain = 1.0
    for dim, shards_of in cuts:
        heights = jax.random.uniform(jax.random.fold_in(jax.random.fold_in(rng, 6), dim), (shards_of,), jnp.float32, smallest / len(cuts), largest / len(cuts))
        gain = gain * jnp.repeat(jnp.exp(heights), extent[dim] // shards_of).reshape((-1,) + (1,) * (len(extent) - 1 - dim))
    return gain


def bell_draw(own_key, extent, spread, most, pieces=(), held_as=jnp.bfloat16):
    array = spread * jax.random.normal(own_key, extent, jnp.float32)
    if pieces:
        array = array * steps_of(own_key, extent, pieces, -0.22, 0.18)
    return jnp.clip(array, -most, most).astype(held_as)


def setup_inputs(seed: int = 0) -> dict:
    splits = jax.random.split(jax.random.key(seed), 12)
    layer_input = bell_draw(splits[0], (TOKENS, D), 1.0, 6.0, ((0, 32),))
    norm1_gain = jnp.clip(1.0 + 0.15 * jax.random.normal(splits[1], (D,), jnp.float32), 0.25, 1.75).astype(jnp.bfloat16)
    norm1_bias = bell_draw(splits[2], (D,), 0.5, 3.0, ((0, 8),))
    qkv_weight = bell_draw(splits[3], (3, D, D), D ** -0.5, 0.125, ((1, 8), (2, 4)))
    qkv_bias = draw_qkv_bias(jax.random.fold_in(splits[11], 71), 0)
    out_weight = bell_draw(splits[5], (D, D), (D // 16) ** -0.5, 0.5, ((0, 4), (1, 8)))
    norm2_gain = jnp.clip(1.0 + 0.15 * jax.random.normal(splits[6], (D,), jnp.float32), 0.25, 1.75).astype(jnp.bfloat16)
    norm2_bias = bell_draw(splits[7], (D,), 0.5, 3.0, ((0, 8),))
    gate_up_weight = bell_draw(splits[8], (2, D, FF), D ** -0.5, 0.125, ((1, 8), (2, 4)))
    down_weight = bell_draw(splits[9], (FF, D), (FF // 4) ** -0.5, 0.15625, ((0, 4), (1, 8)))
    out_cotangent = bell_draw(splits[10], (TOKENS, D), 1.0, 6.0, ((0, 32),))
    return dict(layer_input=layer_input, norm1_gain=norm1_gain, norm1_bias=norm1_bias, qkv_weight=qkv_weight, qkv_bias=qkv_bias, out_weight=out_weight, norm2_gain=norm2_gain, norm2_bias=norm2_bias, gate_up_weight=gate_up_weight, down_weight=down_weight, out_cotangent=out_cotangent)


epsilon = 1e-05

def layer_norm(values):
    row_mean = lax.optimization_barrier(jnp.mean(values, axis=-1, keepdims=True))
    centered = values - row_mean
    inv_sigma = lax.rsqrt(lax.optimization_barrier(jnp.mean(centered * centered, axis=-1, keepdims=True)) + epsilon)
    return (centered * inv_sigma, inv_sigma)

def norm_back(grad_hat, normed, inv_sigma):
    return inv_sigma * (grad_hat - lax.optimization_barrier(jnp.mean(grad_hat, axis=-1, keepdims=True)) - normed * lax.optimization_barrier(jnp.mean(grad_hat * normed, axis=-1, keepdims=True)))

def rotary_tables(length, rot_dims):
    half_rot = rot_dims // 2
    frequency = 10000.0 ** (-(2.0 * jnp.arange(half_rot, dtype=jnp.float32)) / rot_dims)
    angles = jnp.arange(length, dtype=jnp.float32)[:, None] * frequency[None, :]
    return (jnp.cos(angles)[:, None, :], jnp.sin(angles)[:, None, :])

def rotate(tensor, cosine_table, sine_table, rot_dims):
    half_rot = rot_dims // 2
    lower_half = tensor[..., :half_rot]
    upper_half = tensor[..., half_rot:rot_dims]
    return jnp.concatenate([lower_half * cosine_table - upper_half * sine_table, upper_half * cosine_table + lower_half * sine_table, tensor[..., rot_dims:]], axis=-1)

def unrotate(tensor, cosine_table, sine_table, rot_dims):
    half_rot = rot_dims // 2
    lower_half = tensor[..., :half_rot]
    upper_half = tensor[..., half_rot:rot_dims]
    return jnp.concatenate([lower_half * cosine_table + upper_half * sine_table, upper_half * cosine_table - lower_half * sine_table, tensor[..., rot_dims:]], axis=-1)

def causal_mask(length):
    places = jnp.arange(length)
    return places[:, None] >= places[None, :]

def grouped_sum(group_parts):
    rounded = lax.optimization_barrier(group_parts.astype(jnp.bfloat16))
    return lax.optimization_barrier(jnp.sum(rounded.astype(jnp.float32), axis=1))

def reference(layer_input, norm1_gain, norm1_bias, qkv_weight, qkv_bias, out_weight, norm2_gain, norm2_bias, gate_up_weight, down_weight, out_cotangent):
    group_rows = SEQ_DEV * SEQ_LEN
    head_cols = D // N_TENSOR
    unit_cols = FF // N_TENSOR
    score_scale = HEAD_DIM ** (-0.5)
    cosine_table, sine_table = rotary_tables(SEQ_LEN, ROT)
    causal = causal_mask(SEQ_LEN)
    gain_one = norm1_gain.astype(jnp.float32)
    bias_one = norm1_bias.astype(jnp.float32)
    gain_two = norm2_gain.astype(jnp.float32)
    bias_two = norm2_bias.astype(jnp.float32)
    qkv_float = qkv_weight.astype(jnp.float32)
    bias_float = qkv_bias.astype(jnp.float32)
    out_float = out_weight.astype(jnp.float32)
    gate_float = gate_up_weight[0].astype(jnp.float32)
    up_float = gate_up_weight[1].astype(jnp.float32)
    down_float = down_weight.astype(jnp.float32)

    def one_block(totals, inputs):
        x_block, cot_block = inputs
        x_float = x_block.astype(jnp.float32)
        hat_one, inv_one = layer_norm(x_float)
        normed_one = (hat_one * gain_one + bias_one).astype(jnp.bfloat16)
        qkv_all = jnp.einsum('rd,cdk->crk', normed_one.astype(jnp.float32), qkv_float) + bias_float[:, None, :]
        qkv_all = qkv_all.reshape(3, SEQ_DEV, SEQ_LEN, HEADS, HEAD_DIM)
        query_rot = rotate(qkv_all[0], cosine_table, sine_table, ROT).astype(jnp.bfloat16)
        key_rot = rotate(qkv_all[1], cosine_table, sine_table, ROT).astype(jnp.bfloat16)
        value_heads = qkv_all[2].astype(jnp.bfloat16)
        scores = jnp.einsum('sqhd,skhd->shqk', query_rot.astype(jnp.float32), key_rot.astype(jnp.float32)) * score_scale
        scores = jnp.where(causal, scores, -jnp.inf)
        row_top = lax.optimization_barrier(jnp.max(scores, axis=-1, keepdims=True))
        log_total = row_top + jnp.log(lax.optimization_barrier(jnp.sum(jnp.exp(scores - row_top), axis=-1, keepdims=True)))
        prob_full = jnp.exp(scores - log_total)
        prob_low = prob_full.astype(jnp.bfloat16)
        context = jnp.einsum('shqk,skhd->sqhd', prob_low.astype(jnp.float32), value_heads.astype(jnp.float32)).astype(jnp.bfloat16)
        context_rows = context.reshape(group_rows, D)
        attn_out = grouped_sum(jnp.einsum('rtk,tkd->rtd', context_rows.reshape(group_rows, N_TENSOR, head_cols).astype(jnp.float32), out_float.reshape(N_TENSOR, head_cols, D)))
        residual = x_float + attn_out
        hat_two, inv_two = layer_norm(residual)
        normed_two = (hat_two * gain_two + bias_two).astype(jnp.bfloat16)
        gate_proj = jnp.dot(normed_two, gate_up_weight[0], preferred_element_type=jnp.float32)
        up_proj = jnp.dot(normed_two, gate_up_weight[1], preferred_element_type=jnp.float32)
        sigmoid_gate = jax.nn.sigmoid(gate_proj)
        silu_gate = gate_proj * sigmoid_gate
        activation = (silu_gate * up_proj).astype(jnp.bfloat16)
        mlp_out = grouped_sum(jnp.einsum('rtf,tfd->rtd', activation.reshape(group_rows, N_TENSOR, unit_cols).astype(jnp.float32), down_float.reshape(N_TENSOR, unit_cols, D)))
        out_block = (residual + mlp_out).astype(jnp.bfloat16)
        grad_act = jnp.dot(cot_block, down_weight.T, preferred_element_type=jnp.float32)
        grad_gate = (grad_act * up_proj * sigmoid_gate * (1.0 + gate_proj * (1.0 - sigmoid_gate))).astype(jnp.bfloat16)
        grad_up = (grad_act * silu_gate).astype(jnp.bfloat16)
        grad_down = jnp.dot(activation.T, cot_block, preferred_element_type=jnp.float32)
        grad_wgate = jnp.dot(normed_two.T, grad_gate, preferred_element_type=jnp.float32)
        grad_wup = jnp.dot(normed_two.T, grad_up, preferred_element_type=jnp.float32)
        gate_part = jnp.einsum('rtf,dtf->rtd', grad_gate.reshape(group_rows, N_TENSOR, unit_cols).astype(jnp.float32), gate_float.reshape(D, N_TENSOR, unit_cols))
        up_part = jnp.einsum('rtf,dtf->rtd', grad_up.reshape(group_rows, N_TENSOR, unit_cols).astype(jnp.float32), up_float.reshape(D, N_TENSOR, unit_cols))
        grad_normed_two = grouped_sum(gate_part + up_part)
        grad_gain_two = lax.optimization_barrier(jnp.sum(grad_normed_two * hat_two, axis=0))
        grad_bias_two = lax.optimization_barrier(jnp.sum(grad_normed_two, axis=0))
        grad_resid = cot_block.astype(jnp.float32) + norm_back(grad_normed_two * gain_two, hat_two, inv_two)
        grad_resid_low = grad_resid.astype(jnp.bfloat16)
        grad_context = jnp.dot(grad_resid_low, out_weight.T, preferred_element_type=jnp.float32).astype(jnp.bfloat16)
        grad_wout = jnp.dot(context_rows.T, grad_resid_low, preferred_element_type=jnp.float32)
        grad_ctx_heads = grad_context.reshape(SEQ_DEV, SEQ_LEN, HEADS, HEAD_DIM).astype(jnp.float32)
        grad_probs = jnp.einsum('sqhd,skhd->shqk', grad_ctx_heads, value_heads.astype(jnp.float32))
        delta_sum = lax.optimization_barrier(jnp.sum(grad_ctx_heads * context.astype(jnp.float32), axis=-1))
        delta_sum = jnp.transpose(delta_sum, (0, 2, 1))[..., None]
        grad_scores = (prob_full * (grad_probs - delta_sum) * score_scale).astype(jnp.bfloat16).astype(jnp.float32)
        grad_values = jnp.einsum('shqk,sqhd->skhd', prob_low.astype(jnp.float32), grad_ctx_heads)
        grad_query = unrotate(jnp.einsum('shqk,skhd->sqhd', grad_scores, key_rot.astype(jnp.float32)), cosine_table, sine_table, ROT)
        grad_keys = unrotate(jnp.einsum('shqk,sqhd->skhd', grad_scores, query_rot.astype(jnp.float32)), cosine_table, sine_table, ROT)
        grad_pre = jnp.stack([grad_query, grad_keys, grad_values]).reshape(3, group_rows, D).astype(jnp.bfloat16).astype(jnp.float32)
        grad_bqkv = lax.optimization_barrier(jnp.sum(grad_pre, axis=1))
        grad_wqkv = jnp.einsum('rd,crk->cdk', normed_one.astype(jnp.float32), grad_pre)
        grad_normed_one = grouped_sum(jnp.einsum('crtk,cdtk->rtd', grad_pre.reshape(3, group_rows, N_TENSOR, head_cols), qkv_float.reshape(3, D, N_TENSOR, head_cols)))
        grad_gain_one = lax.optimization_barrier(jnp.sum(grad_normed_one * hat_one, axis=0))
        grad_bias_one = lax.optimization_barrier(jnp.sum(grad_normed_one, axis=0))
        grad_in = grad_resid + norm_back(grad_normed_one * gain_one, hat_one, inv_one)
        terms = (grad_gain_one, grad_bias_one, grad_wqkv, grad_bqkv, grad_wout, grad_gain_two, grad_bias_two, grad_wgate, grad_wup, grad_down)
        new_totals = tuple((total + term for total, term in zip(totals, terms)))
        return (new_totals, (out_block, grad_in))
    start_totals = (jnp.zeros((D,), jnp.float32), jnp.zeros((D,), jnp.float32), jnp.zeros((3, D, D), jnp.float32), jnp.zeros((3, D), jnp.float32), jnp.zeros((D, D), jnp.float32), jnp.zeros((D,), jnp.float32), jnp.zeros((D,), jnp.float32), jnp.zeros((D, FF), jnp.float32), jnp.zeros((D, FF), jnp.float32), jnp.zeros((FF, D), jnp.float32))
    blocks_in = (layer_input.reshape(N_DP, group_rows, D), out_cotangent.reshape(N_DP, group_rows, D))
    totals, (out_blocks, grad_blocks) = lax.scan(one_block, start_totals, blocks_in)
    layer_output = out_blocks.reshape(N_DP * group_rows, D)
    grad_input = grad_blocks.reshape(N_DP * group_rows, D)
    grad_gate_up = jnp.stack([totals[7], totals[8]])
    return (layer_output, grad_input, totals[0], totals[1], totals[2], totals[3], totals[4], totals[5], totals[6], grad_gate_up, totals[9])
```

```python
import jax
import jax.numpy as jnp
from jax import lax
from jax.experimental import pallas as pl
from jax.experimental.pallas import tpu as pltpu
from jax.sharding import PartitionSpec as P

HEAD_DIM = 64
ROT = 16
SEQ_LEN = 512
LANES = 128
EPS = 1e-05
F32 = jnp.float32
BF16 = jnp.bfloat16
NT = (((1,), (1,)), ((), ()))
TN = (((0,), (0,)), ((), ()))


def layer_norm(values):
    row_mean = jnp.mean(values, axis=-1, keepdims=True)
    centered = values - row_mean
    inv_sigma = lax.rsqrt(jnp.mean(centered * centered, axis=-1, keepdims=True) + EPS)
    return (centered * inv_sigma, inv_sigma)


def norm_back(grad_hat, normed, inv_sigma):
    return inv_sigma * (
        grad_hat
        - jnp.mean(grad_hat, axis=-1, keepdims=True)
        - normed * jnp.mean(grad_hat * normed, axis=-1, keepdims=True)
    )


def rotary_lanes():
    half = ROT // 2
    frequency = 10000.0 ** (-(2.0 * jnp.arange(half, dtype=F32)) / ROT)
    angles = jnp.arange(SEQ_LEN, dtype=F32)[:, None] * frequency[None, :]
    cosine, sine = jnp.cos(angles), jnp.sin(angles)
    rest = HEAD_DIM - ROT
    zero = jnp.zeros((SEQ_LEN, half), F32)
    tail = jnp.zeros((SEQ_LEN, rest), F32)
    copies = LANES // HEAD_DIM
    keep = jnp.concatenate([cosine, cosine, tail + 1.0] * copies, axis=1)
    low = jnp.concatenate([-sine, zero, tail] * copies, axis=1)
    high = jnp.concatenate([zero, sine, tail] * copies, axis=1)
    return keep, low, high


def bits_of(axis):
    size = lax.axis_size(axis)
    return [1 << b for b in range(size.bit_length() - 1)]


def swap(value, axis, bit):
    return lax.ppermute(value, axis, [(i, i ^ bit) for i in range(lax.axis_size(axis))])


def total_over(value, axis):
    for bit in bits_of(axis):
        value = value + swap(value, axis, bit)
    return value


def row_parts(rows, count):
    tiles = rows // 16
    edges = [16 * (tiles * k // count) for k in range(count)] + [rows]
    return list(zip(edges[:-1], edges[1:]))


def part_plan(rows):
    bits = bits_of("tensor")
    return [
        (lo, hi, bits[k:] + bits[:k]) for k, (lo, hi) in enumerate(row_parts(rows, len(bits)))
    ]


def collect_rows(block):
    rows = block.shape[0]
    pieces = {}
    for lo, hi, order in part_plan(rows):
        held = {0: block[lo:hi]}
        for bit in order:
            held.update({m ^ bit: swap(v, "tensor", bit) for m, v in held.items()})
        for m, v in held.items():
            pieces[(m, lo)] = v
    return jnp.concatenate([pieces[k] for k in sorted(pieces)], axis=0)


def spread_rows(terms, rows):
    done = []
    for lo, hi, order in part_plan(rows):
        held = {m: terms[m * rows + lo : m * rows + hi] for m in range(lax.axis_size("tensor"))}
        for bit in order[::-1]:
            last = bit == order[0]
            nxt = {}
            for m in [m for m in held if not m & bit]:
                total = held[m].astype(F32) + swap(held[m ^ bit], "tensor", bit).astype(F32)
                nxt[m] = total if last else total.astype(BF16)
            held = nxt
        done.append(held[0])
    return jnp.concatenate(done, axis=0)


def ordered(ref, lead, flip, rows):
    return jnp.concatenate(
        [
            ref[lead + (pl.ds(pl.multiple_of((n ^ flip) * rows, rows), rows), slice(None))]
            for n in range(SEQ_LEN // rows)
        ],
        axis=0,
    )


def put_ordered(ref, lead, flip, rows, value):
    for n in range(SEQ_LEN // rows):
        ref[lead + (pl.ds(pl.multiple_of((n ^ flip) * rows, rows), rows), slice(None))] = value[
            n * rows : (n + 1) * rows
        ]


CHUNK = 256
HEADS_STEP = LANES // HEAD_DIM


def lane_roll(value, shift):
    return pltpu.roll(value, shift % LANES, 1)


def masked(scores, start):
    rows = lax.broadcasted_iota(jnp.int32, scores.shape, 0) + start
    cols = lax.broadcasted_iota(jnp.int32, scores.shape, 1)
    return jnp.where(rows >= cols, scores, -jnp.inf)


def attend_kernel(flip_ref, pre_ref, keep_ref, low_ref, high_ref, qkv_ref, ctx_ref, lse_ref, *, rows):
    flip = flip_ref[0]
    half = ROT // 2
    scale = HEAD_DIM ** (-0.5)
    keep, low, high = keep_ref[...], low_ref[...], high_ref[...]
    for c in range(3):
        v = ordered(pre_ref, (c, 0), flip, rows)
        if c < 2:
            v = v * keep + lane_roll(v, -half) * low + lane_roll(v, half) * high
        qkv_ref[c, 0] = v.astype(BF16)
    ctx_parts, lse_parts = [], []
    for start in range(0, SEQ_LEN, CHUNK):
        end = start + CHUNK
        ctxs, lses = [], []
        for h in range(HEADS_STEP):
            cols = slice(h * HEAD_DIM, (h + 1) * HEAD_DIM)
            q = qkv_ref[0, 0, start:end, cols]
            k = qkv_ref[1, 0, :end, cols]
            v = qkv_ref[2, 0, :end, cols]
            s = lax.dot_general(q, k, NT, preferred_element_type=F32) * scale
            s = masked(s, start)
            top = jnp.max(s, axis=-1, keepdims=True)
            e = jnp.exp(s - top)
            total = jnp.sum(e, axis=-1, keepdims=True)
            p = (e * (1.0 / total)).astype(BF16)
            ctxs.append(jnp.dot(p, v, preferred_element_type=F32).astype(BF16))
            lses.append(jnp.broadcast_to(top + jnp.log(total), (CHUNK, HEAD_DIM)))
        ctx_parts.append(jnp.concatenate(ctxs, axis=1))
        lse_parts.append(jnp.concatenate(lses, axis=1))
    put_ordered(ctx_ref, (0,), flip, rows, jnp.concatenate(ctx_parts, axis=0))
    lse_ref[0] = jnp.concatenate(lse_parts, axis=0)


def attend_back_kernel(
    flip_ref, qkv_ref, ctx_ref, gctx_ref, lse_ref, keep_ref, low_ref, high_ref, gpre_ref, bias_ref, *, rows
):
    flip = flip_ref[0]
    half = ROT // 2
    scale = HEAD_DIM ** (-0.5)
    ctx = ordered(ctx_ref, (0,), flip, rows)
    gctx = ordered(gctx_ref, (0,), flip, rows)
    prod = gctx.astype(F32) * ctx.astype(F32)
    starts = list(range(0, SEQ_LEN, CHUNK))
    gq, gk, gv = [], [], []
    for h in range(HEADS_STEP):
        cols = slice(h * HEAD_DIM, (h + 1) * HEAD_DIM)
        dq_parts = []
        dk = [None] * len(starts)
        dv = [None] * len(starts)
        for i, start in enumerate(starts):
            end = start + CHUNK
            q = qkv_ref[0, 0, start:end, cols]
            k = qkv_ref[1, 0, :end, cols]
            v = qkv_ref[2, 0, :end, cols]
            g = gctx[start:end, cols]
            lse = lse_ref[0, start:end, h * HEAD_DIM : h * HEAD_DIM + 1]
            delta = jnp.sum(prod[start:end, cols], axis=-1, keepdims=True)
            s = lax.dot_general(q, k, NT, preferred_element_type=F32) * scale
            p = jnp.exp(masked(s, start) - lse)
            dp = lax.dot_general(g, v, NT, preferred_element_type=F32)
            ds = (p * (dp - delta) * scale).astype(BF16)
            p_low = p.astype(BF16)
            dq_parts.append(jnp.dot(ds, k, preferred_element_type=F32))
            dk_i = lax.dot_general(ds, q, TN, preferred_element_type=F32)
            dv_i = lax.dot_general(p_low, g, TN, preferred_element_type=F32)
            for j in range(i + 1):
                part = slice(j * CHUNK, (j + 1) * CHUNK)
                dk[j] = dk_i[part] if dk[j] is None else dk[j] + dk_i[part]
                dv[j] = dv_i[part] if dv[j] is None else dv[j] + dv_i[part]
        gq.append(jnp.concatenate(dq_parts, axis=0))
        gk.append(jnp.concatenate(dk, axis=0))
        gv.append(jnp.concatenate(dv, axis=0))
    keep, low, high = keep_ref[...], low_ref[...], high_ref[...]
    for c, parts in enumerate((gq, gk, gv)):
        v = jnp.concatenate(parts, axis=1)
        if c < 2:
            v = v * keep - lane_roll(v, -half) * low - lane_roll(v, half) * high
        v = v.astype(BF16)
        put_ordered(gpre_ref, (c, 0), flip, rows, v)
        bias_ref[0, c : c + 1] = jnp.sum(v.astype(F32), axis=0, keepdims=True)


def attend_specs(cols):
    whole = pl.BlockSpec((SEQ_LEN, LANES), lambda s, h, f: (0, 0))
    triple = pl.BlockSpec((3, 1, SEQ_LEN, LANES), lambda s, h, f: (0, s, 0, h))
    single = pl.BlockSpec((1, SEQ_LEN, LANES), lambda s, h, f: (s, 0, h))
    bias = pl.BlockSpec((1, 3, LANES), lambda s, h, f: (s, 0, h))
    return whole, triple, single, bias


def attend(flip, pre, tables, rows):
    import functools

    _, seqs, _, cols = pre.shape
    whole, triple, single, _ = attend_specs(cols)
    return pl.pallas_call(
        functools.partial(attend_kernel, rows=rows),
        out_shape=(
            jax.ShapeDtypeStruct((3, seqs, SEQ_LEN, cols), BF16),
            jax.ShapeDtypeStruct((seqs, SEQ_LEN, cols), BF16),
            jax.ShapeDtypeStruct((seqs, SEQ_LEN, cols), F32),
        ),
        grid_spec=pltpu.PrefetchScalarGridSpec(
            num_scalar_prefetch=1,
            grid=(seqs, cols // LANES),
            in_specs=[triple, whole, whole, whole],
            out_specs=[triple, single, single],
        ),
        name="attend",
    )(flip, pre, *tables)


def attend_back(flip, qkv, ctx, gctx, lse, tables, rows):
    import functools

    _, seqs, _, cols = qkv.shape
    whole, triple, single, bias = attend_specs(cols)
    return pl.pallas_call(
        functools.partial(attend_back_kernel, rows=rows),
        out_shape=(
            jax.ShapeDtypeStruct((3, seqs, SEQ_LEN, cols), BF16),
            jax.ShapeDtypeStruct((seqs, 3, cols), F32),
        ),
        grid_spec=pltpu.PrefetchScalarGridSpec(
            num_scalar_prefetch=1,
            grid=(seqs, cols // LANES),
            in_specs=[triple, single, single, single, whole, whole, whole],
            out_specs=[triple, bias],
        ),
        name="attend_back",
    )(flip, qkv, ctx, gctx, lse, *tables)


def shards(
    layer_input,
    norm1_gain,
    norm1_bias,
    qkv_weight,
    qkv_bias,
    out_weight,
    norm2_gain,
    norm2_bias,
    gate_up_weight,
    down_weight,
    out_cotangent,
):
    rows, width = layer_input.shape
    part = norm1_gain.shape[0]
    dp_count = lax.axis_size("dp")
    dp_here = lax.axis_index("dp")
    blocks = max(SEQ_LEN // rows, 1)
    flip = (lax.axis_index("tensor") & (blocks - 1)).astype(jnp.int32)[None]
    group_rows = rows * lax.axis_size("tensor")
    seqs = group_rows // SEQ_LEN
    head_cols = qkv_weight.shape[2]
    tables = rotary_lanes()

    packed = jnp.concatenate(
        [norm1_gain, norm1_bias, norm2_gain, norm2_bias, qkv_bias.reshape(-1)]
    )
    packed = lax.all_gather(packed, "dp", axis=0, tiled=False)
    gain_one, bias_one, gain_two, bias_two = (
        packed[:, k * part : (k + 1) * part].reshape(width).astype(F32) for k in range(4)
    )
    bias_local = (
        packed[:, 4 * part :].reshape(dp_count, 3, -1).transpose(1, 0, 2).reshape(3, head_cols)
    ).astype(F32)

    qkv_local = lax.all_gather(qkv_weight, "dp", axis=1, tiled=True)
    out_local = lax.all_gather(out_weight, "dp", axis=1, tiled=True)
    gate_up_local = lax.all_gather(gate_up_weight, "dp", axis=1, tiled=True)
    down_local = lax.all_gather(down_weight, "dp", axis=1, tiled=True)

    x_float = layer_input.astype(F32)
    hat_one, inv_one = layer_norm(x_float)
    rows_one = collect_rows((hat_one * gain_one + bias_one).astype(BF16))
    pre = (
        jnp.einsum("rd,cdk->crk", rows_one, qkv_local, preferred_element_type=F32)
        + bias_local[:, None, :]
    )
    qkv_heads, context, lse = attend(
        flip, pre.reshape(3, seqs, SEQ_LEN, head_cols), tables, min(rows, SEQ_LEN)
    )
    context_rows = context.reshape(group_rows, head_cols)
    attn_terms = jnp.dot(context_rows, out_local, preferred_element_type=F32).astype(BF16)
    residual = x_float + spread_rows(attn_terms, rows)

    hat_two, inv_two = layer_norm(residual)
    rows_two = collect_rows((hat_two * gain_two + bias_two).astype(BF16))
    cot_rows = collect_rows(out_cotangent)
    gate_proj = jnp.dot(rows_two, gate_up_local[0], preferred_element_type=F32)
    up_proj = jnp.dot(rows_two, gate_up_local[1], preferred_element_type=F32)
    sigmoid_gate = jax.nn.sigmoid(gate_proj)
    silu_gate = gate_proj * sigmoid_gate
    activation = (silu_gate * up_proj).astype(BF16)
    mlp_terms = jnp.dot(activation, down_local, preferred_element_type=F32).astype(BF16)
    layer_output = (residual + spread_rows(mlp_terms, rows)).astype(BF16)

    grad_act = lax.dot_general(cot_rows, down_local, NT, preferred_element_type=F32)
    grad_gate = (
        grad_act * up_proj * sigmoid_gate * (1.0 + gate_proj * (1.0 - sigmoid_gate))
    ).astype(BF16)
    grad_up = (grad_act * silu_gate).astype(BF16)
    back_terms = (
        lax.dot_general(grad_gate, gate_up_local[0], NT, preferred_element_type=F32)
        + lax.dot_general(grad_up, gate_up_local[1], NT, preferred_element_type=F32)
    ).astype(BF16)
    grad_down = lax.dot_general(activation, cot_rows, TN, preferred_element_type=F32)
    grad_wgate = lax.dot_general(rows_two, grad_gate, TN, preferred_element_type=F32)
    grad_wup = lax.dot_general(rows_two, grad_up, TN, preferred_element_type=F32)
    share_down = lax.psum_scatter(
        grad_down.astype(BF16), "dp", scatter_dimension=1, tiled=True
    ).astype(F32)
    share_gate = lax.psum_scatter(
        grad_wgate.astype(BF16), "dp", scatter_dimension=0, tiled=True
    ).astype(F32)
    share_up = lax.psum_scatter(
        grad_wup.astype(BF16), "dp", scatter_dimension=0, tiled=True
    ).astype(F32)
    grad_normed_two = spread_rows(back_terms, rows)
    grad_resid = out_cotangent.astype(F32) + norm_back(
        grad_normed_two * gain_two, hat_two, inv_two
    )

    resid_rows = collect_rows(grad_resid.astype(BF16))
    grad_context = lax.dot_general(
        resid_rows, out_local, NT, preferred_element_type=F32
    ).astype(BF16)
    grad_pre, bias_sums = attend_back(
        flip,
        qkv_heads,
        context,
        grad_context.reshape(seqs, SEQ_LEN, head_cols),
        lse,
        tables,
        min(rows, SEQ_LEN),
    )
    grad_pre = grad_pre.reshape(3, group_rows, head_cols)
    qkv_terms = jnp.einsum(
        "crk,cdk->rd", grad_pre, qkv_local, preferred_element_type=F32
    ).astype(BF16)
    grad_wout = lax.dot_general(context_rows, resid_rows, TN, preferred_element_type=F32)
    grad_wqkv = jnp.einsum("rd,crk->cdk", rows_one, grad_pre, preferred_element_type=F32)
    share_out = lax.psum_scatter(
        grad_wout.astype(BF16), "dp", scatter_dimension=1, tiled=True
    ).astype(F32)
    share_qkv = lax.psum_scatter(
        grad_wqkv.astype(BF16), "dp", scatter_dimension=1, tiled=True
    ).astype(F32)
    grad_normed_one = spread_rows(qkv_terms, rows)
    grad_input = grad_resid + norm_back(grad_normed_one * gain_one, hat_one, inv_one)

    bias_total = total_over(jnp.sum(bias_sums, axis=0), "dp")
    bias_part = qkv_bias.shape[1]
    share_bias = lax.dynamic_slice_in_dim(bias_total, dp_here * bias_part, bias_part, axis=1)
    norm_sums = jnp.stack(
        [
            jnp.sum(grad_normed_one * hat_one, axis=0),
            jnp.sum(grad_normed_one, axis=0),
            jnp.sum(grad_normed_two * hat_two, axis=0),
            jnp.sum(grad_normed_two, axis=0),
        ]
    )
    norm_total = total_over(total_over(norm_sums, "tensor"), "dp")
    share_norm = lax.dynamic_slice_in_dim(norm_total, dp_here * part, part, axis=1)
    return (
        layer_output,
        grad_input,
        share_norm[0],
        share_norm[1],
        share_qkv,
        share_bias,
        share_out,
        share_norm[2],
        share_norm[3],
        jnp.stack([share_gate, share_up]),
        share_down,
    )


def solution(mesh):
    placed = (
        P(("dp", "tensor"), None),
        P("dp"),
        P("dp"),
        P(None, "dp", "tensor"),
        P(None, ("tensor", "dp")),
        P("tensor", "dp"),
        P("dp"),
        P("dp"),
        P(None, "dp", "tensor"),
        P("tensor", "dp"),
        P(("dp", "tensor"), None),
    )
    return jax.shard_map(
        shards,
        mesh=mesh,
        in_specs=placed,
        out_specs=(
            P(("dp", "tensor"), None),
            P(("dp", "tensor"), None),
            P("dp"),
            P("dp"),
            P(None, "dp", "tensor"),
            P(None, ("tensor", "dp")),
            P("tensor", "dp"),
            P("dp"),
            P("dp"),
            P(None, "dp", "tensor"),
            P("tensor", "dp"),
        ),
        check_vma=False,
    )
```

```python
import functools

import jax
import jax.numpy as jnp
from jax import lax
from jax.experimental import pallas as pl
from jax.experimental.pallas import tpu as pltpu
from jax.sharding import PartitionSpec as P

HEAD_DIM = 64
ROT = 16
SEQ_LEN = 512
LANES = 128
EPS = 1e-05
F32 = jnp.float32
BF16 = jnp.bfloat16
NT = (((1,), (1,)), ((), ()))
TN = (((0,), (0,)), ((), ()))


def layer_norm(values):
    row_mean = jnp.mean(values, axis=-1, keepdims=True)
    centered = values - row_mean
    inv_sigma = lax.rsqrt(jnp.mean(centered * centered, axis=-1, keepdims=True) + EPS)
    return (centered * inv_sigma, inv_sigma)


def norm_back(grad_hat, normed, inv_sigma):
    return inv_sigma * (
        grad_hat
        - jnp.mean(grad_hat, axis=-1, keepdims=True)
        - normed * jnp.mean(grad_hat * normed, axis=-1, keepdims=True)
    )


def rotary_lanes():
    half = ROT // 2
    frequency = 10000.0 ** (-(2.0 * jnp.arange(half, dtype=F32)) / ROT)
    angles = jnp.arange(SEQ_LEN, dtype=F32)[:, None] * frequency[None, :]
    cosine, sine = jnp.cos(angles), jnp.sin(angles)
    rest = HEAD_DIM - ROT
    zero = jnp.zeros((SEQ_LEN, half), F32)
    tail = jnp.zeros((SEQ_LEN, rest), F32)
    copies = LANES // HEAD_DIM
    keep = jnp.concatenate([cosine, cosine, tail + 1.0] * copies, axis=1)
    low = jnp.concatenate([-sine, zero, tail] * copies, axis=1)
    high = jnp.concatenate([zero, sine, tail] * copies, axis=1)
    return keep, low, high


def bits_of(axis):
    size = lax.axis_size(axis)
    return [1 << b for b in range(size.bit_length() - 1)]


def swap(value, axis, bit):
    return lax.ppermute(value, axis, [(i, i ^ bit) for i in range(lax.axis_size(axis))])


def total_over(value, axis):
    for bit in bits_of(axis):
        value = value + swap(value, axis, bit)
    return value


def row_parts(rows, count):
    tiles = rows // 16
    edges = [16 * (tiles * k // count) for k in range(count)] + [rows]
    return list(zip(edges[:-1], edges[1:]))


def part_plan(rows):
    bits = bits_of("tensor")
    return [
        (lo, hi, bits[k:] + bits[:k]) for k, (lo, hi) in enumerate(row_parts(rows, len(bits)))
    ]


def collect_rows(block):
    parts = []
    for lo, hi, order in part_plan(block.shape[0]):
        held = block[lo:hi]
        for bit in order:
            held = jnp.concatenate([held, swap(held, "tensor", bit)], axis=0)
        parts.append(held)
    return jnp.concatenate(parts, axis=0)


def spread_part(terms, order):
    held = terms
    for bit in order[::-1]:
        half = held.shape[0] // 2
        got = swap(held[half:], "tensor", bit)
        total = held[:half].astype(F32) + got.astype(F32)
        held = total if bit == order[0] else total.astype(BF16)
    return held


def spread_rows(term_fn, group, rows):
    count = lax.axis_size("tensor")
    return jnp.concatenate(
        [
            spread_part(term_fn(slice(lo * count, hi * count)), order)
            for lo, hi, order in part_plan(rows)
        ],
        axis=0,
    )


def frame_pieces(rows):
    count = lax.axis_size("tensor")
    per_seq = SEQ_LEN // rows
    return [
        (member, lo, hi, order)
        for member in range(count)
        for lo, hi, order in part_plan(rows)
    ], per_seq * len(part_plan(rows))


def frame_offsets(rows):
    count = lax.axis_size("tensor")
    here = lax.axis_index("tensor").astype(jnp.int32)
    places = []
    for member, lo, hi, order in frame_pieces(rows)[0]:
        other = here ^ member
        place = jnp.int32(0)
        for j, bit in enumerate(order):
            place = place + jnp.where((other & bit) != 0, 1 << j, 0)
        places.append(lo * count + place * (hi - lo))
    return jnp.stack(places).astype(jnp.int32)


def ring_step(value):
    count = lax.axis_size("dp")
    return lax.ppermute(value, "dp", [(i, (i + 2) % count) for i in range(count)])


def ring_gather(shard, axis):
    count = lax.axis_size("dp")
    here = lax.axis_index("dp")
    size = shard.shape[axis]
    full = jnp.zeros(shard.shape[:axis] + (size * count,) + shard.shape[axis + 1 :], shard.dtype)
    seen = []
    held = shard
    for k in range(count // 2):
        if k:
            held = ring_step(held)
        seen.append(held)
        owner = (here - 2 * k) % count
        full = lax.dynamic_update_slice_in_dim(full, held, owner * size, axis)
        full = lax.dynamic_update_slice_in_dim(full, swap(held, "dp", 1), (owner ^ 1) * size, axis)
    return full, seen


def ring_reduce(grad, axis):
    count = lax.axis_size("dp")
    here = lax.axis_index("dp")
    size = grad.shape[axis] // count
    lead, tail = grad.shape[:axis], grad.shape[axis + 1 :]
    pairs = grad.reshape(lead + (count // 2, 2, size) + tail)
    core = here % 2
    mine = lax.dynamic_index_in_dim(pairs, core, axis + 1, keepdims=False)
    other = lax.dynamic_index_in_dim(pairs, 1 - core, axis + 1, keepdims=False)
    other = swap(other, "dp", 1)

    def block(k):
        owner = (here // 2 - k) % (count // 2)
        return lax.dynamic_index_in_dim(mine, owner, axis, keepdims=False).astype(
            F32
        ) + lax.dynamic_index_in_dim(other, owner, axis, keepdims=False).astype(F32)

    total = block(1)
    for k in list(range(2, count // 2)) + [0]:
        total = block(k) + ring_step(total.astype(BF16)).astype(F32)
    return total


def after(value, *others):
    return lax.optimization_barrier((value,) + others)[0]


def ordered(ref, lead, offs_ref, runs):
    return jnp.concatenate(
        [
            ref[lead + (pl.ds(pl.multiple_of(offs_ref[i], 16), size), slice(None))]
            for i, size in runs
        ],
        axis=0,
    )


def put_ordered(ref, lead, offs_ref, runs, value):
    at = 0
    for i, size in runs:
        ref[lead + (pl.ds(pl.multiple_of(offs_ref[i], 16), size), slice(None))] = value[
            at : at + size
        ]
        at += size


CHUNK = 256
HEADS_STEP = LANES // HEAD_DIM


def lane_roll(value, shift):
    return pltpu.roll(value, shift % LANES, 1)


def masked(scores, start):
    rows = lax.broadcasted_iota(jnp.int32, scores.shape, 0) + start
    cols = lax.broadcasted_iota(jnp.int32, scores.shape, 1)
    return jnp.where(rows >= cols, scores, -jnp.inf)


def attend_kernel(offs_ref, pre_ref, keep_ref, low_ref, high_ref, qkv_ref, ctx_ref, lse_ref, *, runs):
    for seq, seq_runs in enumerate(runs):
        attend_seq(
            offs_ref, pre_ref, keep_ref, low_ref, high_ref, qkv_ref, ctx_ref, lse_ref, seq, seq_runs
        )


def attend_seq(
    offs_ref, pre_ref, keep_ref, low_ref, high_ref, qkv_ref, ctx_ref, lse_ref, seq, runs
):
    half = ROT // 2
    scale = HEAD_DIM ** (-0.5)
    keep, low, high = keep_ref[...], low_ref[...], high_ref[...]
    for c in range(3):
        v = ordered(pre_ref, (c,), offs_ref, runs)
        if c < 2:
            v = v * keep + lane_roll(v, -half) * low + lane_roll(v, half) * high
        qkv_ref[c, seq] = v.astype(BF16)
    ctx_parts, lse_parts = [], []
    for start in range(0, SEQ_LEN, CHUNK):
        end = start + CHUNK
        ctxs, lses = [], []
        for h in range(HEADS_STEP):
            cols = slice(h * HEAD_DIM, (h + 1) * HEAD_DIM)
            q = qkv_ref[0, seq, start:end, cols]
            k = qkv_ref[1, seq, :end, cols]
            v = qkv_ref[2, seq, :end, cols]
            s = lax.dot_general(q, k, NT, preferred_element_type=F32) * scale
            s = masked(s, start)
            top = jnp.max(s, axis=-1, keepdims=True)
            e = jnp.exp(s - top)
            total = jnp.sum(e, axis=-1, keepdims=True)
            p = (e * (1.0 / total)).astype(BF16)
            ctxs.append(jnp.dot(p, v, preferred_element_type=F32).astype(BF16))
            lses.append(jnp.broadcast_to(top + jnp.log(total), (CHUNK, HEAD_DIM)))
        ctx_parts.append(jnp.concatenate(ctxs, axis=1))
        lse_parts.append(jnp.concatenate(lses, axis=1))
    put_ordered(ctx_ref, (), offs_ref, runs, jnp.concatenate(ctx_parts, axis=0))
    lse_ref[seq] = jnp.concatenate(lse_parts, axis=0)


def attend_back_kernel(offs_ref, *refs, runs):
    for seq, seq_runs in enumerate(runs):
        attend_back_seq(offs_ref, *refs, seq, seq_runs)


def attend_back_seq(
    offs_ref,
    qkv_ref,
    ctx_ref,
    gctx_ref,
    lse_ref,
    keep_ref,
    low_ref,
    high_ref,
    gpre_ref,
    bias_ref,
    seq,
    runs,
):
    half = ROT // 2
    scale = HEAD_DIM ** (-0.5)
    ctx = ordered(ctx_ref, (), offs_ref, runs)
    gctx = ordered(gctx_ref, (), offs_ref, runs)
    prod = gctx.astype(F32) * ctx.astype(F32)
    starts = list(range(0, SEQ_LEN, CHUNK))
    gq, gk, gv = [], [], []
    for h in range(HEADS_STEP):
        cols = slice(h * HEAD_DIM, (h + 1) * HEAD_DIM)
        dq_parts = []
        dk = [None] * len(starts)
        dv = [None] * len(starts)
        for i, start in enumerate(starts):
            end = start + CHUNK
            q = qkv_ref[0, seq, start:end, cols]
            k = qkv_ref[1, seq, :end, cols]
            v = qkv_ref[2, seq, :end, cols]
            g = gctx[start:end, cols]
            lse = lse_ref[seq, start:end, h * HEAD_DIM : h * HEAD_DIM + 1]
            delta = jnp.sum(prod[start:end, cols], axis=-1, keepdims=True)
            s = lax.dot_general(q, k, NT, preferred_element_type=F32) * scale
            p = jnp.exp(masked(s, start) - lse)
            dp = lax.dot_general(g, v, NT, preferred_element_type=F32)
            ds = (p * (dp - delta) * scale).astype(BF16)
            p_low = p.astype(BF16)
            dq_parts.append(jnp.dot(ds, k, preferred_element_type=F32))
            dk_i = lax.dot_general(ds, q, TN, preferred_element_type=F32)
            dv_i = lax.dot_general(p_low, g, TN, preferred_element_type=F32)
            for j in range(i + 1):
                part = slice(j * CHUNK, (j + 1) * CHUNK)
                dk[j] = dk_i[part] if dk[j] is None else dk[j] + dk_i[part]
                dv[j] = dv_i[part] if dv[j] is None else dv[j] + dv_i[part]
        gq.append(jnp.concatenate(dq_parts, axis=0))
        gk.append(jnp.concatenate(dk, axis=0))
        gv.append(jnp.concatenate(dv, axis=0))
    keep, low, high = keep_ref[...], low_ref[...], high_ref[...]
    for c, parts in enumerate((gq, gk, gv)):
        v = jnp.concatenate(parts, axis=1)
        if c < 2:
            v = v * keep - lane_roll(v, -half) * low - lane_roll(v, half) * high
        v = v.astype(BF16)
        put_ordered(gpre_ref, (c,), offs_ref, runs, v)
        bias_ref[seq, c : c + 1] = jnp.sum(v.astype(F32), axis=0, keepdims=True)


def attend_specs(seqs, group_rows):
    table = pl.BlockSpec((SEQ_LEN, LANES), lambda h, f: (0, 0))
    framed3 = pl.BlockSpec((3, group_rows, LANES), lambda h, f: (0, 0, h))
    framed = pl.BlockSpec((group_rows, LANES), lambda h, f: (0, h))
    natural3 = pl.BlockSpec((3, seqs, SEQ_LEN, LANES), lambda h, f: (0, 0, 0, h))
    natural = pl.BlockSpec((seqs, SEQ_LEN, LANES), lambda h, f: (0, 0, h))
    bias = pl.BlockSpec((seqs, 3, LANES), lambda h, f: (0, 0, h))
    return table, framed3, framed, natural3, natural, bias


def sequence_runs(rows):
    pieces, per_seq = frame_pieces(rows)
    runs = [(i, hi - lo) for i, (_, lo, hi, _) in enumerate(pieces)]
    return tuple(tuple(runs[i : i + per_seq]) for i in range(0, len(runs), per_seq))


def attend(offs, pre, tables, runs):
    _, group_rows, cols = pre.shape
    seqs = group_rows // SEQ_LEN
    table, framed3, framed, natural3, natural, _ = attend_specs(seqs, group_rows)
    return pl.pallas_call(
        functools.partial(attend_kernel, runs=runs),
        out_shape=(
            jax.ShapeDtypeStruct((3, seqs, SEQ_LEN, cols), BF16),
            jax.ShapeDtypeStruct((group_rows, cols), BF16),
            jax.ShapeDtypeStruct((seqs, SEQ_LEN, cols), F32),
        ),
        grid_spec=pltpu.PrefetchScalarGridSpec(
            num_scalar_prefetch=1,
            grid=(cols // LANES,),
            in_specs=[framed3, table, table, table],
            out_specs=[natural3, framed, natural],
        ),
        name="attend",
    )(offs, pre, *tables)


def attend_back(offs, qkv, ctx, gctx, lse, tables, runs):
    _, seqs, _, cols = qkv.shape
    group_rows = seqs * SEQ_LEN
    table, framed3, framed, natural3, natural, bias = attend_specs(seqs, group_rows)
    return pl.pallas_call(
        functools.partial(attend_back_kernel, runs=runs),
        out_shape=(
            jax.ShapeDtypeStruct((3, group_rows, cols), BF16),
            jax.ShapeDtypeStruct((seqs, 3, cols), F32),
        ),
        grid_spec=pltpu.PrefetchScalarGridSpec(
            num_scalar_prefetch=1,
            grid=(cols // LANES,),
            in_specs=[natural3, framed, framed, natural, table, table, table],
            out_specs=[framed3, bias],
        ),
        name="attend_back",
    )(offs, qkv, ctx, gctx, lse, *tables)


def shards(
    layer_input,
    norm1_gain,
    norm1_bias,
    qkv_weight,
    qkv_bias,
    out_weight,
    norm2_gain,
    norm2_bias,
    gate_up_weight,
    down_weight,
    out_cotangent,
):
    rows, width = layer_input.shape
    part = norm1_gain.shape[0]
    dp_count = lax.axis_size("dp")
    dp_here = lax.axis_index("dp")
    group_rows = rows * lax.axis_size("tensor")
    head_cols = qkv_weight.shape[2]
    offs = frame_offsets(rows)
    runs = sequence_runs(rows)
    tables = rotary_lanes()

    packed = jnp.concatenate(
        [norm1_gain, norm1_bias, norm2_gain, norm2_bias, qkv_bias.reshape(-1)]
    )[None]
    for bit in bits_of("dp"):
        packed = jnp.concatenate([packed, swap(packed, "dp", bit)], axis=0)
    packed = jnp.take(packed, jnp.arange(dp_count) ^ dp_here, axis=0)
    gain_one, bias_one, gain_two, bias_two = (
        packed[:, k * part : (k + 1) * part].reshape(width).astype(F32) for k in range(4)
    )
    bias_local = (
        packed[:, 4 * part :].reshape(dp_count, 3, -1).transpose(1, 0, 2).reshape(3, head_cols)
    ).astype(F32)

    qkv_local, qkv_seen = ring_gather(qkv_weight, 1)
    out_local = lax.all_gather(after(out_weight, qkv_seen[-2]), "dp", axis=1, tiled=True)
    gate_up_local = lax.all_gather(after(gate_up_weight, qkv_seen[-1]), "dp", axis=1, tiled=True)
    down_turned, _ = ring_gather(after(down_weight.T, qkv_seen[-1]), 0)

    x_float = layer_input.astype(F32)
    hat_one, inv_one = layer_norm(x_float)
    rows_one = collect_rows((hat_one * gain_one + bias_one).astype(BF16))
    cot_rows = collect_rows(after(out_cotangent, rows_one))
    pre = (
        jnp.einsum("rd,cdk->crk", rows_one, qkv_local, preferred_element_type=F32)
        + bias_local[:, None, :]
    )
    qkv_heads, context, lse = attend(offs, pre, tables, runs)
    residual = x_float + spread_rows(
        lambda at: jnp.dot(context[at], out_local, preferred_element_type=F32).astype(BF16),
        context,
        rows,
    )

    hat_two, inv_two = layer_norm(residual)
    rows_two = collect_rows((hat_two * gain_two + bias_two).astype(BF16))
    gate_proj = jnp.dot(rows_two, gate_up_local[0], preferred_element_type=F32)
    up_proj = jnp.dot(rows_two, gate_up_local[1], preferred_element_type=F32)
    sigmoid_gate = jax.nn.sigmoid(gate_proj)
    silu_gate = gate_proj * sigmoid_gate
    activation = (silu_gate * up_proj).astype(BF16)

    grad_down = lax.dot_general(cot_rows, activation, TN, preferred_element_type=F32)
    share_down = ring_reduce(grad_down.astype(BF16), 0).T
    grad_act = jnp.dot(cot_rows, down_turned, preferred_element_type=F32)
    grad_gate = (
        grad_act * up_proj * sigmoid_gate * (1.0 + gate_proj * (1.0 - sigmoid_gate))
    ).astype(BF16)
    grad_up = (grad_act * silu_gate).astype(BF16)
    grad_normed_two = spread_rows(
        lambda at: (
            lax.dot_general(grad_gate[at], gate_up_local[0], NT, preferred_element_type=F32)
            + lax.dot_general(grad_up[at], gate_up_local[1], NT, preferred_element_type=F32)
        ).astype(BF16),
        grad_gate,
        rows,
    )
    grad_wgate = lax.dot_general(
        rows_two, grad_gate, TN, preferred_element_type=F32
    ).astype(BF16)
    grad_wup = lax.dot_general(rows_two, grad_up, TN, preferred_element_type=F32).astype(BF16)
    share_gate = lax.psum_scatter(grad_wgate, "dp", scatter_dimension=0, tiled=True).astype(F32)
    share_up = lax.psum_scatter(grad_wup, "dp", scatter_dimension=0, tiled=True).astype(F32)
    grad_normed_two = after(grad_normed_two, grad_wgate, grad_wup)
    grad_resid = out_cotangent.astype(F32) + norm_back(
        grad_normed_two * gain_two, hat_two, inv_two
    )

    resid_rows = collect_rows(grad_resid.astype(BF16))
    late_act = after(activation, resid_rows)
    layer_output = (
        residual
        + spread_rows(
            lambda at: lax.dot_general(
                late_act[at], down_turned, NT, preferred_element_type=F32
            ).astype(BF16),
            activation,
            rows,
        )
    ).astype(BF16)
    grad_context = lax.dot_general(
        resid_rows, out_local, NT, preferred_element_type=F32
    ).astype(BF16)
    grad_pre, bias_sums = attend_back(offs, qkv_heads, context, grad_context, lse, tables, runs)
    grad_wqkv = jnp.einsum(
        "rd,crk->cdk", rows_one, grad_pre, preferred_element_type=F32
    ).astype(BF16)
    share_qkv = ring_reduce(grad_wqkv, 1)
    late_pre = after(grad_pre, grad_wqkv)
    grad_normed_one = spread_rows(
        lambda at: jnp.einsum(
            "crk,cdk->rd", late_pre[:, at], qkv_local, preferred_element_type=F32
        ).astype(BF16),
        grad_pre,
        rows,
    )
    grad_wout = lax.dot_general(context, resid_rows, TN, preferred_element_type=F32)
    share_out = lax.psum_scatter(
        grad_wout.astype(BF16), "dp", scatter_dimension=1, tiled=True
    ).astype(F32)
    grad_input = grad_resid + norm_back(grad_normed_one * gain_one, hat_one, inv_one)

    bias_total = total_over(jnp.sum(bias_sums, axis=0), "dp")
    bias_part = qkv_bias.shape[1]
    share_bias = lax.dynamic_slice_in_dim(bias_total, dp_here * bias_part, bias_part, axis=1)
    norm_sums = jnp.stack(
        [
            jnp.sum(grad_normed_one * hat_one, axis=0),
            jnp.sum(grad_normed_one, axis=0),
            jnp.sum(grad_normed_two * hat_two, axis=0),
            jnp.sum(grad_normed_two, axis=0),
        ]
    )
    norm_total = total_over(total_over(norm_sums, "tensor"), "dp")
    share_norm = lax.dynamic_slice_in_dim(norm_total, dp_here * part, part, axis=1)
    return (
        layer_output,
        grad_input,
        share_norm[0],
        share_norm[1],
        share_qkv,
        share_bias,
        share_out,
        share_norm[2],
        share_norm[3],
        jnp.stack([share_gate, share_up]),
        share_down,
    )


def solution(mesh):
    placed = (
        P(("dp", "tensor"), None),
        P("dp"),
        P("dp"),
        P(None, "dp", "tensor"),
        P(None, ("tensor", "dp")),
        P("tensor", "dp"),
        P("dp"),
        P("dp"),
        P(None, "dp", "tensor"),
        P("tensor", "dp"),
        P(("dp", "tensor"), None),
    )
    return jax.shard_map(
        shards,
        mesh=mesh,
        in_specs=placed,
        out_specs=(
            P(("dp", "tensor"), None),
            P(("dp", "tensor"), None),
            P("dp"),
            P("dp"),
            P(None, "dp", "tensor"),
            P(None, ("tensor", "dp")),
            P("tensor", "dp"),
            P("dp"),
            P("dp"),
            P(None, "dp", "tensor"),
            P("tensor", "dp"),
        ),
        check_vma=False,
    )
```

```python
import functools

import jax
import jax.numpy as jnp
from jax import lax
from jax.experimental import pallas as pl
from jax.experimental.pallas import tpu as pltpu
from jax.sharding import PartitionSpec as P


HEAD_DIM = 64
ROT = 16
SEQ_LEN = 512
LANES = 128
EPS = 1e-05
F32 = jnp.float32
BF16 = jnp.bfloat16
NT = (((1,), (1,)), ((), ()))
TN = (((0,), (0,)), ((), ()))


def layer_norm(values):
    row_mean = jnp.mean(values, axis=-1, keepdims=True)
    centered = values - row_mean
    inv_sigma = lax.rsqrt(jnp.mean(centered * centered, axis=-1, keepdims=True) + EPS)
    return (centered * inv_sigma, inv_sigma)


def norm_back(grad_hat, normed, inv_sigma):
    return inv_sigma * (
        grad_hat
        - jnp.mean(grad_hat, axis=-1, keepdims=True)
        - normed * jnp.mean(grad_hat * normed, axis=-1, keepdims=True)
    )


def rotary_lanes():
    half = ROT // 2
    frequency = 10000.0 ** (-(2.0 * jnp.arange(half, dtype=F32)) / ROT)
    angles = jnp.arange(SEQ_LEN, dtype=F32)[:, None] * frequency[None, :]
    cosine, sine = jnp.cos(angles), jnp.sin(angles)
    rest = HEAD_DIM - ROT
    zero = jnp.zeros((SEQ_LEN, half), F32)
    tail = jnp.zeros((SEQ_LEN, rest), F32)
    copies = LANES // HEAD_DIM
    keep = jnp.concatenate([cosine, cosine, tail + 1.0] * copies, axis=1)
    low = jnp.concatenate([-sine, zero, tail] * copies, axis=1)
    high = jnp.concatenate([zero, sine, tail] * copies, axis=1)
    return keep, low, high


def bits_of(axis):
    size = lax.axis_size(axis)
    return [1 << b for b in range(size.bit_length() - 1)]


def swap(value, axis, bit):
    return lax.ppermute(value, axis, [(i, i ^ bit) for i in range(lax.axis_size(axis))])


def total_over(value, axis):
    for bit in bits_of(axis):
        value = value + swap(value, axis, bit)
    return value


def row_parts(rows, count):
    tiles = rows // 16
    edges = [16 * (tiles * k // count) for k in range(count)] + [rows]
    return list(zip(edges[:-1], edges[1:]))


def part_plan(rows):
    bits = bits_of("tensor")
    return [
        (lo, hi, bits[k:] + bits[:k]) for k, (lo, hi) in enumerate(row_parts(rows, len(bits)))
    ]


def collect_rows(block):
    parts = []
    for lo, hi, order in part_plan(block.shape[0]):
        held = block[lo:hi]
        for bit in order:
            held = jnp.concatenate([held, swap(held, "tensor", bit)], axis=0)
        parts.append(held)
    return jnp.concatenate(parts, axis=0)


def spread_part(terms, order):
    held = terms
    for bit in order[::-1]:
        half = held.shape[0] // 2
        got = swap(held[half:], "tensor", bit)
        total = held[:half].astype(F32) + got.astype(F32)
        held = total if bit == order[0] else total.astype(BF16)
    return held


def part_slices(rows):
    count = lax.axis_size("tensor")
    return [slice(lo * count, hi * count) for lo, hi, _ in part_plan(rows)]


def spread_rows(terms, rows):
    return jnp.concatenate(
        [spread_part(t, order) for t, (_, _, order) in zip(terms, part_plan(rows))], axis=0
    )


def frame_pieces(rows):
    count = lax.axis_size("tensor")
    per_seq = SEQ_LEN // rows
    return [
        (member, lo, hi, order)
        for member in range(count)
        for lo, hi, order in part_plan(rows)
    ], per_seq * len(part_plan(rows))


def frame_offsets(rows):
    count = lax.axis_size("tensor")
    here = lax.axis_index("tensor").astype(jnp.int32)
    places = []
    for member, lo, hi, order in frame_pieces(rows)[0]:
        other = here ^ member
        place = jnp.int32(0)
        for j, bit in enumerate(order):
            place = place + jnp.where((other & bit) != 0, 1 << j, 0)
        places.append(lo * count + place * (hi - lo))
    return jnp.stack(places).astype(jnp.int32)


def after(value, *others):
    return lax.optimization_barrier((value,) + others)[0]


def ordered(ref, lead, offs_ref, runs):
    return jnp.concatenate(
        [
            ref[lead + (pl.ds(pl.multiple_of(offs_ref[i], 16), size), slice(None))]
            for i, size in runs
        ],
        axis=0,
    )


def put_ordered(ref, lead, offs_ref, runs, value):
    at = 0
    for i, size in runs:
        ref[lead + (pl.ds(pl.multiple_of(offs_ref[i], 16), size), slice(None))] = value[
            at : at + size
        ]
        at += size


CHUNK = 256
HEADS_STEP = LANES // HEAD_DIM


def lane_roll(value, shift):
    return pltpu.roll(value, shift % LANES, 1)


def masked(scores, start):
    rows = lax.broadcasted_iota(jnp.int32, scores.shape, 0) + start
    cols = lax.broadcasted_iota(jnp.int32, scores.shape, 1)
    return jnp.where(rows >= cols, scores, -jnp.inf)


def attend_kernel(offs_ref, pre_ref, keep_ref, low_ref, high_ref, qkv_ref, ctx_ref, lse_ref, *, runs):
    for seq, seq_runs in enumerate(runs):
        attend_seq(
            offs_ref, pre_ref, keep_ref, low_ref, high_ref, qkv_ref, ctx_ref, lse_ref, seq, seq_runs
        )


def attend_seq(
    offs_ref, pre_ref, keep_ref, low_ref, high_ref, qkv_ref, ctx_ref, lse_ref, seq, runs
):
    half = ROT // 2
    scale = HEAD_DIM ** (-0.5)
    keep, low, high = keep_ref[...], low_ref[...], high_ref[...]
    for c in range(3):
        v = ordered(pre_ref, (c,), offs_ref, runs)
        if c < 2:
            v = v * keep + lane_roll(v, -half) * low + lane_roll(v, half) * high
        qkv_ref[c, seq] = v.astype(BF16)
    ctx_parts, lse_parts = [], []
    for start in range(0, SEQ_LEN, CHUNK):
        end = start + CHUNK
        ctxs, lses = [], []
        for h in range(HEADS_STEP):
            cols = slice(h * HEAD_DIM, (h + 1) * HEAD_DIM)
            q = qkv_ref[0, seq, start:end, cols]
            k = qkv_ref[1, seq, :end, cols]
            v = qkv_ref[2, seq, :end, cols]
            s = lax.dot_general(q, k, NT, preferred_element_type=F32) * scale
            s = masked(s, start)
            top = jnp.max(s, axis=-1, keepdims=True)
            e = jnp.exp(s - top)
            total = jnp.sum(e, axis=-1, keepdims=True)
            p = (e * (1.0 / total)).astype(BF16)
            ctxs.append(jnp.dot(p, v, preferred_element_type=F32).astype(BF16))
            lses.append(jnp.broadcast_to(top + jnp.log(total), (CHUNK, HEAD_DIM)))
        ctx_parts.append(jnp.concatenate(ctxs, axis=1))
        lse_parts.append(jnp.concatenate(lses, axis=1))
    put_ordered(ctx_ref, (), offs_ref, runs, jnp.concatenate(ctx_parts, axis=0))
    lse_ref[seq] = jnp.concatenate(lse_parts, axis=0)


def attend_back_kernel(offs_ref, *refs, runs):
    for seq, seq_runs in enumerate(runs):
        attend_back_seq(offs_ref, *refs, seq, seq_runs)


def attend_back_seq(
    offs_ref,
    qkv_ref,
    ctx_ref,
    gctx_ref,
    lse_ref,
    keep_ref,
    low_ref,
    high_ref,
    gpre_ref,
    bias_ref,
    seq,
    runs,
):
    half = ROT // 2
    scale = HEAD_DIM ** (-0.5)
    ctx = ordered(ctx_ref, (), offs_ref, runs)
    gctx = ordered(gctx_ref, (), offs_ref, runs)
    prod = gctx.astype(F32) * ctx.astype(F32)
    starts = list(range(0, SEQ_LEN, CHUNK))
    gq, gk, gv = [], [], []
    for h in range(HEADS_STEP):
        cols = slice(h * HEAD_DIM, (h + 1) * HEAD_DIM)
        dq_parts = []
        dk = [None] * len(starts)
        dv = [None] * len(starts)
        for i, start in enumerate(starts):
            end = start + CHUNK
            q = qkv_ref[0, seq, start:end, cols]
            k = qkv_ref[1, seq, :end, cols]
            v = qkv_ref[2, seq, :end, cols]
            g = gctx[start:end, cols]
            lse = lse_ref[seq, start:end, h * HEAD_DIM : h * HEAD_DIM + 1]
            delta = jnp.sum(prod[start:end, cols], axis=-1, keepdims=True)
            s = lax.dot_general(q, k, NT, preferred_element_type=F32) * scale
            p = jnp.exp(masked(s, start) - lse)
            dp = lax.dot_general(g, v, NT, preferred_element_type=F32)
            ds = (p * (dp - delta) * scale).astype(BF16)
            p_low = p.astype(BF16)
            dq_parts.append(jnp.dot(ds, k, preferred_element_type=F32))
            dk_i = lax.dot_general(ds, q, TN, preferred_element_type=F32)
            dv_i = lax.dot_general(p_low, g, TN, preferred_element_type=F32)
            for j in range(i + 1):
                part = slice(j * CHUNK, (j + 1) * CHUNK)
                dk[j] = dk_i[part] if dk[j] is None else dk[j] + dk_i[part]
                dv[j] = dv_i[part] if dv[j] is None else dv[j] + dv_i[part]
        gq.append(jnp.concatenate(dq_parts, axis=0))
        gk.append(jnp.concatenate(dk, axis=0))
        gv.append(jnp.concatenate(dv, axis=0))
    keep, low, high = keep_ref[...], low_ref[...], high_ref[...]
    for c, parts in enumerate((gq, gk, gv)):
        v = jnp.concatenate(parts, axis=1)
        if c < 2:
            v = v * keep - lane_roll(v, -half) * low - lane_roll(v, half) * high
        v = v.astype(BF16)
        put_ordered(gpre_ref, (c,), offs_ref, runs, v)
        bias_ref[seq, c : c + 1] = jnp.sum(v.astype(F32), axis=0, keepdims=True)


def attend_specs(seqs, group_rows):
    table = pl.BlockSpec((SEQ_LEN, LANES), lambda h, f: (0, 0))
    framed3 = pl.BlockSpec((3, group_rows, LANES), lambda h, f: (0, 0, h))
    framed = pl.BlockSpec((group_rows, LANES), lambda h, f: (0, h))
    natural3 = pl.BlockSpec((3, seqs, SEQ_LEN, LANES), lambda h, f: (0, 0, 0, h))
    natural = pl.BlockSpec((seqs, SEQ_LEN, LANES), lambda h, f: (0, 0, h))
    bias = pl.BlockSpec((seqs, 3, LANES), lambda h, f: (0, 0, h))
    return table, framed3, framed, natural3, natural, bias


def sequence_runs(rows):
    pieces, per_seq = frame_pieces(rows)
    runs = [(i, hi - lo) for i, (_, lo, hi, _) in enumerate(pieces)]
    return tuple(tuple(runs[i : i + per_seq]) for i in range(0, len(runs), per_seq))


def attend(offs, pre, tables, runs):
    _, group_rows, cols = pre.shape
    seqs = group_rows // SEQ_LEN
    table, framed3, framed, natural3, natural, _ = attend_specs(seqs, group_rows)
    return pl.pallas_call(
        functools.partial(attend_kernel, runs=runs),
        out_shape=(
            jax.ShapeDtypeStruct((3, seqs, SEQ_LEN, cols), BF16),
            jax.ShapeDtypeStruct((group_rows, cols), BF16),
            jax.ShapeDtypeStruct((seqs, SEQ_LEN, cols), F32),
        ),
        grid_spec=pltpu.PrefetchScalarGridSpec(
            num_scalar_prefetch=1,
            grid=(cols // LANES,),
            in_specs=[framed3, table, table, table],
            out_specs=[natural3, framed, natural],
        ),
        name="attend",
    )(offs, pre, *tables)


def attend_back(offs, qkv, ctx, gctx, lse, tables, runs):
    _, seqs, _, cols = qkv.shape
    group_rows = seqs * SEQ_LEN
    table, framed3, framed, natural3, natural, bias = attend_specs(seqs, group_rows)
    return pl.pallas_call(
        functools.partial(attend_back_kernel, runs=runs),
        out_shape=(
            jax.ShapeDtypeStruct((3, group_rows, cols), BF16),
            jax.ShapeDtypeStruct((seqs, 3, cols), F32),
        ),
        grid_spec=pltpu.PrefetchScalarGridSpec(
            num_scalar_prefetch=1,
            grid=(cols // LANES,),
            in_specs=[natural3, framed, framed, natural, table, table, table],
            out_specs=[framed3, bias],
        ),
        name="attend_back",
    )(offs, qkv, ctx, gctx, lse, *tables)


def shards(
    layer_input,
    norm1_gain,
    norm1_bias,
    qkv_weight,
    qkv_bias,
    out_weight,
    norm2_gain,
    norm2_bias,
    gate_up_weight,
    down_weight,
    out_cotangent,
):
    rows, width = layer_input.shape
    part = norm1_gain.shape[0]
    dp_count = lax.axis_size("dp")
    dp_here = lax.axis_index("dp")
    head_cols = qkv_weight.shape[2]
    offs = frame_offsets(rows)
    runs = sequence_runs(rows)
    tables = rotary_lanes()

    attn_shard = jnp.concatenate([qkv_weight, out_weight.T[None]], axis=0)
    attn_local = lax.all_gather(attn_shard, "dp", axis=1, tiled=True)
    qkv_local, out_turned = attn_local[:3], attn_local[3]
    gate_up_local = lax.all_gather(gate_up_weight, "dp", axis=1, tiled=True)
    down_local = lax.all_gather(down_weight, "dp", axis=1, tiled=True)

    x_rows = collect_rows(layer_input)
    packed = jnp.concatenate(
        [norm1_gain, norm1_bias, norm2_gain, norm2_bias, qkv_bias.reshape(-1)]
    )
    packed = lax.all_gather(packed, "dp", axis=0, tiled=False)
    gain_one, bias_one, gain_two, bias_two = (
        packed[:, k * part : (k + 1) * part].reshape(width).astype(F32) for k in range(4)
    )
    bias_local = (
        packed[:, 4 * part :].reshape(dp_count, 3, -1).transpose(1, 0, 2).reshape(3, head_cols)
    ).astype(F32)

    x_float = layer_input.astype(F32)
    hat_one, inv_one = layer_norm(x_float)
    rows_one = (layer_norm(x_rows.astype(F32))[0] * gain_one + bias_one).astype(BF16)
    pre = (
        jnp.einsum("rd,cdk->crk", rows_one, qkv_local, preferred_element_type=F32)
        + bias_local[:, None, :]
    )
    qkv_heads, context, lse = attend(offs, pre, tables, runs)
    parts = part_slices(rows)
    attn_terms = [
        lax.dot_general(context[at], out_turned, NT, preferred_element_type=F32).astype(BF16)
        for at in parts
    ]
    residual = x_float + spread_rows(attn_terms, rows)
    cot_rows = collect_rows(after(out_cotangent, rows_one))

    hat_two, inv_two = layer_norm(residual)
    rows_two = collect_rows((hat_two * gain_two + bias_two).astype(BF16))
    gate_proj = jnp.dot(rows_two, gate_up_local[0], preferred_element_type=F32)
    up_proj = jnp.dot(rows_two, gate_up_local[1], preferred_element_type=F32)
    sigmoid_gate = jax.nn.sigmoid(gate_proj)
    silu_gate = gate_proj * sigmoid_gate
    activation = (silu_gate * up_proj).astype(BF16)

    grad_down = lax.dot_general(
        activation, cot_rows, TN, preferred_element_type=F32
    ).astype(BF16)
    share_down = lax.psum_scatter(grad_down, "dp", scatter_dimension=1, tiled=True)
    share_down = share_down.astype(F32)
    grad_act = lax.dot_general(
        after(cot_rows, grad_down), down_local, NT, preferred_element_type=F32
    )
    grad_gate = (
        grad_act * up_proj * sigmoid_gate * (1.0 + gate_proj * (1.0 - sigmoid_gate))
    ).astype(BF16)
    grad_up = (grad_act * silu_gate).astype(BF16)
    back_terms = [
        (
            lax.dot_general(grad_gate[at], gate_up_local[0], NT, preferred_element_type=F32)
            + lax.dot_general(grad_up[at], gate_up_local[1], NT, preferred_element_type=F32)
        ).astype(BF16)
        for at in parts
    ]
    grad_normed_two = spread_rows(back_terms, rows)
    grad_gate_up = jnp.stack([grad_gate, grad_up])
    grad_wgate_up = jnp.einsum(
        "rd,crk->cdk",
        after(rows_two, *back_terms),
        grad_gate_up,
        preferred_element_type=F32,
    ).astype(BF16)
    share_gate_up = lax.psum_scatter(grad_wgate_up, "dp", scatter_dimension=1, tiled=True)
    share_gate_up = share_gate_up.astype(F32)
    grad_normed_two, _, mlp_act = lax.optimization_barrier(
        (grad_normed_two, grad_wgate_up, activation)
    )
    grad_resid = out_cotangent.astype(F32) + norm_back(
        grad_normed_two * gain_two, hat_two, inv_two
    )

    mlp_terms = jnp.dot(mlp_act, down_local, preferred_element_type=F32).astype(BF16)
    resid_rows, mlp_terms = lax.optimization_barrier(
        (collect_rows(grad_resid.astype(BF16)), mlp_terms)
    )
    grad_context = jnp.dot(resid_rows, out_turned, preferred_element_type=F32).astype(BF16)
    grad_pre, bias_sums = attend_back(offs, qkv_heads, context, grad_context, lse, tables, runs)
    grad_wqkv = jnp.einsum(
        "rd,crk->cdk", rows_one, grad_pre, preferred_element_type=F32
    ).astype(BF16)
    grad_wout = lax.dot_general(
        resid_rows, context, TN, preferred_element_type=F32
    ).astype(BF16)
    grad_wattn = jnp.concatenate([grad_wqkv, grad_wout[None]], axis=0)
    share_attn = lax.psum_scatter(grad_wattn, "dp", scatter_dimension=1, tiled=True)
    share_attn = share_attn.astype(F32)
    late_pre = after(grad_pre, grad_wattn)
    qkv_terms = [
        jnp.einsum(
            "crk,cdk->rd", late_pre[:, at], qkv_local, preferred_element_type=F32
        ).astype(BF16)
        for at in parts
    ]
    grad_normed_one = spread_rows(qkv_terms, rows)
    grad_input = grad_resid + norm_back(grad_normed_one * gain_one, hat_one, inv_one)
    layer_output = (residual + spread_rows([mlp_terms[at] for at in parts], rows)).astype(BF16)

    norm_sums = jnp.stack(
        [
            jnp.sum(grad_normed_one * hat_one, axis=0),
            jnp.sum(grad_normed_one, axis=0),
            jnp.sum(grad_normed_two * hat_two, axis=0),
            jnp.sum(grad_normed_two, axis=0),
        ]
    )
    norm_total = total_over(norm_sums, "tensor").reshape(-1)
    bias_total = jnp.sum(bias_sums, axis=0).reshape(-1)
    totals = total_over(jnp.concatenate([norm_total, bias_total]), "dp")
    norm_total = totals[: 4 * width].reshape(4, width)
    bias_total = totals[4 * width :].reshape(3, head_cols)
    share_norm = lax.dynamic_slice_in_dim(norm_total, dp_here * part, part, axis=1)
    bias_part = qkv_bias.shape[1]
    share_bias = lax.dynamic_slice_in_dim(bias_total, dp_here * bias_part, bias_part, axis=1)
    return (
        layer_output,
        grad_input,
        share_norm[0],
        share_norm[1],
        share_attn[:3],
        share_bias,
        share_attn[3].T,
        share_norm[2],
        share_norm[3],
        share_gate_up,
        share_down,
    )


def solution(mesh):
    placed = (
        P(("dp", "tensor"), None),
        P("dp"),
        P("dp"),
        P(None, "dp", "tensor"),
        P(None, ("tensor", "dp")),
        P("tensor", "dp"),
        P("dp"),
        P("dp"),
        P(None, "dp", "tensor"),
        P("tensor", "dp"),
        P(("dp", "tensor"), None),
    )

    return jax.shard_map(
        shards,
        mesh=mesh,
        in_specs=placed,
        out_specs=(
            P(("dp", "tensor"), None),
            P(("dp", "tensor"), None),
            P("dp"),
            P("dp"),
            P(None, "dp", "tensor"),
            P(None, ("tensor", "dp")),
            P("tensor", "dp"),
            P("dp"),
            P("dp"),
            P(None, "dp", "tensor"),
            P("tensor", "dp"),
        ),
        check_vma=False,
    )
```

```python
import functools

import jax
import jax.numpy as jnp
from jax import lax
from jax.experimental import pallas as pl
from jax.experimental.pallas import tpu as pltpu
from jax.sharding import PartitionSpec as P


HEAD_DIM = 64
ROT = 16
SEQ_LEN = 512
LANES = 128
EPS = 1e-05
F32 = jnp.float32
BF16 = jnp.bfloat16
NT = (((1,), (1,)), ((), ()))
TN = (((0,), (0,)), ((), ()))


def layer_norm(values):
    row_mean = jnp.mean(values, axis=-1, keepdims=True)
    centered = values - row_mean
    inv_sigma = lax.rsqrt(jnp.mean(centered * centered, axis=-1, keepdims=True) + EPS)
    return (centered * inv_sigma, inv_sigma)


def norm_back(grad_hat, normed, inv_sigma):
    return inv_sigma * (
        grad_hat
        - jnp.mean(grad_hat, axis=-1, keepdims=True)
        - normed * jnp.mean(grad_hat * normed, axis=-1, keepdims=True)
    )


def rotary_lanes():
    half = ROT // 2
    frequency = 10000.0 ** (-(2.0 * jnp.arange(half, dtype=F32)) / ROT)
    angles = jnp.arange(SEQ_LEN, dtype=F32)[:, None] * frequency[None, :]
    cosine, sine = jnp.cos(angles), jnp.sin(angles)
    rest = HEAD_DIM - ROT
    zero = jnp.zeros((SEQ_LEN, half), F32)
    tail = jnp.zeros((SEQ_LEN, rest), F32)
    copies = LANES // HEAD_DIM
    keep = jnp.concatenate([cosine, cosine, tail + 1.0] * copies, axis=1)
    low = jnp.concatenate([-sine, zero, tail] * copies, axis=1)
    high = jnp.concatenate([zero, sine, tail] * copies, axis=1)
    return keep, low, high


def bits_of(axis):
    size = lax.axis_size(axis)
    return [1 << b for b in range(size.bit_length() - 1)]


def swap(value, axis, bit):
    return lax.ppermute(value, axis, [(i, i ^ bit) for i in range(lax.axis_size(axis))])


def total_over(value, axis):
    for bit in bits_of(axis):
        value = value + swap(value, axis, bit)
    return value


def row_parts(rows, count):
    tiles = rows // 16
    edges = [16 * (tiles * k // count) for k in range(count)] + [rows]
    return list(zip(edges[:-1], edges[1:]))


def part_plan(rows):
    bits = bits_of("tensor")
    return [
        (lo, hi, bits[k:] + bits[:k]) for k, (lo, hi) in enumerate(row_parts(rows, len(bits)))
    ]


def together(values):
    return list(lax.optimization_barrier(tuple(values)))


def collect_rows(block):
    plan = part_plan(block.shape[0])
    held = [block[lo:hi] for lo, hi, _ in plan]
    for j in range(len(plan)):
        got = [swap(h, "tensor", order[j]) for h, (_, _, order) in zip(held, plan)]
        held = together(jnp.concatenate([h, g], axis=0) for h, g in zip(held, got))
    return jnp.concatenate(held, axis=0)


def part_slices(rows):
    count = lax.axis_size("tensor")
    return [slice(lo * count, hi * count) for lo, hi, _ in part_plan(rows)]


def spread_rows(terms, rows):
    plan = part_plan(rows)
    held = list(terms)
    for j in reversed(range(len(plan))):
        totals = []
        for h, (_, _, order) in zip(held, plan):
            half = h.shape[0] // 2
            got = swap(h[half:], "tensor", order[j])
            total = h[:half].astype(F32) + got.astype(F32)
            totals.append(total.astype(BF16) if j else total)
        held = together(totals)
    return jnp.concatenate(held, axis=0)


def frame_pieces(rows):
    count = lax.axis_size("tensor")
    per_seq = SEQ_LEN // rows
    return [
        (member, lo, hi, order)
        for member in range(count)
        for lo, hi, order in part_plan(rows)
    ], per_seq * len(part_plan(rows))


def frame_offsets(rows):
    count = lax.axis_size("tensor")
    here = lax.axis_index("tensor").astype(jnp.int32)
    places = []
    for member, lo, hi, order in frame_pieces(rows)[0]:
        other = here ^ member
        place = jnp.int32(0)
        for j, bit in enumerate(order):
            place = place + jnp.where((other & bit) != 0, 1 << j, 0)
        places.append(lo * count + place * (hi - lo))
    return jnp.stack(places).astype(jnp.int32)


def after(value, *others):
    return lax.optimization_barrier((value,) + others)[0]


def ordered(ref, lead, offs_ref, runs):
    return jnp.concatenate(
        [
            ref[lead + (pl.ds(pl.multiple_of(offs_ref[i], 16), size), slice(None))]
            for i, size in runs
        ],
        axis=0,
    )


def put_ordered(ref, lead, offs_ref, runs, value):
    at = 0
    for i, size in runs:
        ref[lead + (pl.ds(pl.multiple_of(offs_ref[i], 16), size), slice(None))] = value[
            at : at + size
        ]
        at += size


CHUNK = 256
HEADS_STEP = LANES // HEAD_DIM


def lane_roll(value, shift):
    return pltpu.roll(value, shift % LANES, 1)


def masked(scores, start):
    rows = lax.broadcasted_iota(jnp.int32, scores.shape, 0) + start
    cols = lax.broadcasted_iota(jnp.int32, scores.shape, 1)
    return jnp.where(rows >= cols, scores, -jnp.inf)


def attend_kernel(offs_ref, pre_ref, keep_ref, low_ref, high_ref, qkv_ref, ctx_ref, lse_ref, *, runs):
    for seq, seq_runs in enumerate(runs):
        attend_seq(
            offs_ref, pre_ref, keep_ref, low_ref, high_ref, qkv_ref, ctx_ref, lse_ref, seq, seq_runs
        )


def attend_seq(
    offs_ref, pre_ref, keep_ref, low_ref, high_ref, qkv_ref, ctx_ref, lse_ref, seq, runs
):
    half = ROT // 2
    scale = HEAD_DIM ** (-0.5)
    keep, low, high = keep_ref[...], low_ref[...], high_ref[...]
    for c in range(3):
        v = ordered(pre_ref, (c,), offs_ref, runs)
        if c < 2:
            v = v * keep + lane_roll(v, -half) * low + lane_roll(v, half) * high
        qkv_ref[c, seq] = v.astype(BF16)
    ctx_parts, lse_parts = [], []
    for start in range(0, SEQ_LEN, CHUNK):
        end = start + CHUNK
        ctxs, lses = [], []
        for h in range(HEADS_STEP):
            cols = slice(h * HEAD_DIM, (h + 1) * HEAD_DIM)
            q = qkv_ref[0, seq, start:end, cols]
            k = qkv_ref[1, seq, :end, cols]
            v = qkv_ref[2, seq, :end, cols]
            s = lax.dot_general(q, k, NT, preferred_element_type=F32) * scale
            s = masked(s, start)
            top = jnp.max(s, axis=-1, keepdims=True)
            e = jnp.exp(s - top)
            total = jnp.sum(e, axis=-1, keepdims=True)
            p = (e * (1.0 / total)).astype(BF16)
            ctxs.append(jnp.dot(p, v, preferred_element_type=F32).astype(BF16))
            lses.append(jnp.broadcast_to(top + jnp.log(total), (CHUNK, HEAD_DIM)))
        ctx_parts.append(jnp.concatenate(ctxs, axis=1))
        lse_parts.append(jnp.concatenate(lses, axis=1))
    put_ordered(ctx_ref, (), offs_ref, runs, jnp.concatenate(ctx_parts, axis=0))
    lse_ref[seq] = jnp.concatenate(lse_parts, axis=0)


def attend_back_kernel(offs_ref, *refs, runs):
    for seq, seq_runs in enumerate(runs):
        attend_back_seq(offs_ref, *refs, seq, seq_runs)


def attend_back_seq(
    offs_ref,
    qkv_ref,
    ctx_ref,
    gctx_ref,
    lse_ref,
    keep_ref,
    low_ref,
    high_ref,
    gpre_ref,
    bias_ref,
    seq,
    runs,
):
    half = ROT // 2
    scale = HEAD_DIM ** (-0.5)
    ctx = ordered(ctx_ref, (), offs_ref, runs)
    gctx = ordered(gctx_ref, (), offs_ref, runs)
    prod = gctx.astype(F32) * ctx.astype(F32)
    starts = list(range(0, SEQ_LEN, CHUNK))
    gq, gk, gv = [], [], []
    for h in range(HEADS_STEP):
        cols = slice(h * HEAD_DIM, (h + 1) * HEAD_DIM)
        dq_parts = []
        dk = [None] * len(starts)
        dv = [None] * len(starts)
        for i, start in enumerate(starts):
            end = start + CHUNK
            q = qkv_ref[0, seq, start:end, cols]
            k = qkv_ref[1, seq, :end, cols]
            v = qkv_ref[2, seq, :end, cols]
            g = gctx[start:end, cols]
            lse = lse_ref[seq, start:end, h * HEAD_DIM : h * HEAD_DIM + 1]
            delta = jnp.sum(prod[start:end, cols], axis=-1, keepdims=True)
            s = lax.dot_general(q, k, NT, preferred_element_type=F32) * scale
            p = jnp.exp(masked(s, start) - lse)
            dp = lax.dot_general(g, v, NT, preferred_element_type=F32)
            ds = (p * (dp - delta) * scale).astype(BF16)
            p_low = p.astype(BF16)
            dq_parts.append(jnp.dot(ds, k, preferred_element_type=F32))
            dk_i = lax.dot_general(ds, q, TN, preferred_element_type=F32)
            dv_i = lax.dot_general(p_low, g, TN, preferred_element_type=F32)
            for j in range(i + 1):
                part = slice(j * CHUNK, (j + 1) * CHUNK)
                dk[j] = dk_i[part] if dk[j] is None else dk[j] + dk_i[part]
                dv[j] = dv_i[part] if dv[j] is None else dv[j] + dv_i[part]
        gq.append(jnp.concatenate(dq_parts, axis=0))
        gk.append(jnp.concatenate(dk, axis=0))
        gv.append(jnp.concatenate(dv, axis=0))
    keep, low, high = keep_ref[...], low_ref[...], high_ref[...]
    for c, parts in enumerate((gq, gk, gv)):
        v = jnp.concatenate(parts, axis=1)
        if c < 2:
            v = v * keep - lane_roll(v, -half) * low - lane_roll(v, half) * high
        v = v.astype(BF16)
        put_ordered(gpre_ref, (c,), offs_ref, runs, v)
        bias_ref[seq, c : c + 1] = jnp.sum(v.astype(F32), axis=0, keepdims=True)


def attend_specs(seqs, group_rows):
    table = pl.BlockSpec((SEQ_LEN, LANES), lambda h, f: (0, 0))
    framed3 = pl.BlockSpec((3, group_rows, LANES), lambda h, f: (0, 0, h))
    framed = pl.BlockSpec((group_rows, LANES), lambda h, f: (0, h))
    natural3 = pl.BlockSpec((3, seqs, SEQ_LEN, LANES), lambda h, f: (0, 0, 0, h))
    natural = pl.BlockSpec((seqs, SEQ_LEN, LANES), lambda h, f: (0, 0, h))
    bias = pl.BlockSpec((seqs, 3, LANES), lambda h, f: (0, 0, h))
    return table, framed3, framed, natural3, natural, bias


def sequence_runs(rows):
    pieces, per_seq = frame_pieces(rows)
    runs = [(i, hi - lo) for i, (_, lo, hi, _) in enumerate(pieces)]
    return tuple(tuple(runs[i : i + per_seq]) for i in range(0, len(runs), per_seq))


def attend(offs, pre, tables, runs):
    _, group_rows, cols = pre.shape
    seqs = group_rows // SEQ_LEN
    table, framed3, framed, natural3, natural, _ = attend_specs(seqs, group_rows)
    return pl.pallas_call(
        functools.partial(attend_kernel, runs=runs),
        out_shape=(
            jax.ShapeDtypeStruct((3, seqs, SEQ_LEN, cols), BF16),
            jax.ShapeDtypeStruct((group_rows, cols), BF16),
            jax.ShapeDtypeStruct((seqs, SEQ_LEN, cols), F32),
        ),
        grid_spec=pltpu.PrefetchScalarGridSpec(
            num_scalar_prefetch=1,
            grid=(cols // LANES,),
            in_specs=[framed3, table, table, table],
            out_specs=[natural3, framed, natural],
        ),
        name="attend",
    )(offs, pre, *tables)


def attend_back(offs, qkv, ctx, gctx, lse, tables, runs):
    _, seqs, _, cols = qkv.shape
    group_rows = seqs * SEQ_LEN
    table, framed3, framed, natural3, natural, bias = attend_specs(seqs, group_rows)
    return pl.pallas_call(
        functools.partial(attend_back_kernel, runs=runs),
        out_shape=(
            jax.ShapeDtypeStruct((3, group_rows, cols), BF16),
            jax.ShapeDtypeStruct((seqs, 3, cols), F32),
        ),
        grid_spec=pltpu.PrefetchScalarGridSpec(
            num_scalar_prefetch=1,
            grid=(cols // LANES,),
            in_specs=[natural3, framed, framed, natural, table, table, table],
            out_specs=[framed3, bias],
        ),
        name="attend_back",
    )(offs, qkv, ctx, gctx, lse, *tables)


def shards(
    layer_input,
    norm1_gain,
    norm1_bias,
    qkv_weight,
    qkv_bias,
    out_weight,
    norm2_gain,
    norm2_bias,
    gate_up_weight,
    down_weight,
    out_cotangent,
):
    rows, width = layer_input.shape
    part = norm1_gain.shape[0]
    dp_count = lax.axis_size("dp")
    dp_here = lax.axis_index("dp")
    head_cols = qkv_weight.shape[2]
    offs = frame_offsets(rows)
    runs = sequence_runs(rows)
    tables = rotary_lanes()

    attn_shard = jnp.concatenate([qkv_weight, out_weight.T[None]], axis=0)
    attn_local = lax.all_gather(attn_shard, "dp", axis=1, tiled=True)
    qkv_local, out_turned = attn_local[:3], attn_local[3]
    gate_up_local = lax.all_gather(gate_up_weight, "dp", axis=1, tiled=True)
    down_local = lax.all_gather(down_weight, "dp", axis=1, tiled=True)

    x_rows = collect_rows(layer_input)
    cot_rows = collect_rows(after(out_cotangent, x_rows))
    packed = jnp.concatenate(
        [norm1_gain, norm1_bias, norm2_gain, norm2_bias, qkv_bias.reshape(-1)]
    )
    packed = lax.all_gather(after(packed, x_rows), "dp", axis=0, tiled=False)
    gain_one, bias_one, gain_two, bias_two = (
        packed[:, k * part : (k + 1) * part].reshape(width).astype(F32) for k in range(4)
    )
    bias_local = (
        packed[:, 4 * part :].reshape(dp_count, 3, -1).transpose(1, 0, 2).reshape(3, head_cols)
    ).astype(F32)

    x_float = layer_input.astype(F32)
    hat_one, inv_one = layer_norm(x_float)
    rows_one = (layer_norm(x_rows.astype(F32))[0] * gain_one + bias_one).astype(BF16)
    pre = (
        jnp.einsum("rd,cdk->crk", rows_one, qkv_local, preferred_element_type=F32)
        + bias_local[:, None, :]
    )
    qkv_heads, context, lse = attend(offs, after(pre, cot_rows), tables, runs)
    parts = part_slices(rows)
    attn_terms = [
        lax.dot_general(context[at], out_turned, NT, preferred_element_type=F32).astype(BF16)
        for at in parts
    ]
    residual = x_float + spread_rows(attn_terms, rows)

    hat_two, inv_two = layer_norm(residual)
    rows_two = collect_rows((hat_two * gain_two + bias_two).astype(BF16))
    gate_proj = jnp.dot(rows_two, gate_up_local[0], preferred_element_type=F32)
    up_proj = jnp.dot(rows_two, gate_up_local[1], preferred_element_type=F32)
    sigmoid_gate = jax.nn.sigmoid(gate_proj)
    silu_gate = gate_proj * sigmoid_gate
    activation = (silu_gate * up_proj).astype(BF16)

    grad_down = lax.dot_general(
        activation, cot_rows, TN, preferred_element_type=F32
    ).astype(BF16)
    share_down = lax.psum_scatter(grad_down, "dp", scatter_dimension=1, tiled=True)
    share_down = share_down.astype(F32)
    grad_act = lax.dot_general(
        after(cot_rows, grad_down), down_local, NT, preferred_element_type=F32
    )
    grad_gate = (
        grad_act * up_proj * sigmoid_gate * (1.0 + gate_proj * (1.0 - sigmoid_gate))
    ).astype(BF16)
    grad_up = (grad_act * silu_gate).astype(BF16)
    back_terms = [
        (
            lax.dot_general(grad_gate[at], gate_up_local[0], NT, preferred_element_type=F32)
            + lax.dot_general(grad_up[at], gate_up_local[1], NT, preferred_element_type=F32)
        ).astype(BF16)
        for at in parts
    ]
    grad_normed_two = spread_rows(back_terms, rows)
    grad_gate_up = jnp.stack([grad_gate, grad_up])
    grad_wgate_up = jnp.einsum(
        "rd,crk->cdk",
        after(rows_two, *back_terms),
        grad_gate_up,
        preferred_element_type=F32,
    ).astype(BF16)
    share_gate_up = lax.psum_scatter(grad_wgate_up, "dp", scatter_dimension=1, tiled=True)
    share_gate_up = share_gate_up.astype(F32)
    grad_normed_two, _, mlp_act = lax.optimization_barrier(
        (grad_normed_two, grad_wgate_up, activation)
    )
    grad_resid = out_cotangent.astype(F32) + norm_back(
        grad_normed_two * gain_two, hat_two, inv_two
    )

    mlp_terms = jnp.dot(mlp_act, down_local, preferred_element_type=F32).astype(BF16)
    resid_rows, mlp_terms = lax.optimization_barrier(
        (collect_rows(grad_resid.astype(BF16)), mlp_terms)
    )
    grad_context = jnp.dot(resid_rows, out_turned, preferred_element_type=F32).astype(BF16)
    grad_pre, bias_sums = attend_back(offs, qkv_heads, context, grad_context, lse, tables, runs)
    grad_wqkv = jnp.einsum(
        "rd,crk->cdk", rows_one, grad_pre, preferred_element_type=F32
    ).astype(BF16)
    grad_wout = lax.dot_general(
        resid_rows, context, TN, preferred_element_type=F32
    ).astype(BF16)
    grad_wattn = jnp.concatenate([grad_wqkv, grad_wout[None]], axis=0)
    share_attn = lax.psum_scatter(grad_wattn, "dp", scatter_dimension=1, tiled=True)
    share_attn = share_attn.astype(F32)
    layer_output = (residual + spread_rows([mlp_terms[at] for at in parts], rows)).astype(BF16)
    late_pre, layer_output = lax.optimization_barrier((grad_pre, layer_output, grad_wattn))[:2]
    qkv_terms = [
        jnp.einsum(
            "crk,cdk->rd", late_pre[:, at], qkv_local, preferred_element_type=F32
        ).astype(BF16)
        for at in parts
    ]
    grad_normed_one = spread_rows(qkv_terms, rows)
    grad_input = grad_resid + norm_back(grad_normed_one * gain_one, hat_one, inv_one)

    norm_sums = jnp.stack(
        [
            jnp.sum(grad_normed_one * hat_one, axis=0),
            jnp.sum(grad_normed_one, axis=0),
            jnp.sum(grad_normed_two * hat_two, axis=0),
            jnp.sum(grad_normed_two, axis=0),
        ]
    )
    norm_total = total_over(norm_sums, "tensor").reshape(-1)
    bias_total = jnp.sum(bias_sums, axis=0).reshape(-1)
    totals = total_over(jnp.concatenate([norm_total, bias_total]), "dp")
    norm_total = totals[: 4 * width].reshape(4, width)
    bias_total = totals[4 * width :].reshape(3, head_cols)
    share_norm = lax.dynamic_slice_in_dim(norm_total, dp_here * part, part, axis=1)
    bias_part = qkv_bias.shape[1]
    share_bias = lax.dynamic_slice_in_dim(bias_total, dp_here * bias_part, bias_part, axis=1)
    return (
        layer_output,
        grad_input,
        share_norm[0],
        share_norm[1],
        share_attn[:3],
        share_bias,
        share_attn[3].T,
        share_norm[2],
        share_norm[3],
        share_gate_up,
        share_down,
    )


def solution(mesh):
    placed = (
        P(("dp", "tensor"), None),
        P("dp"),
        P("dp"),
        P(None, "dp", "tensor"),
        P(None, ("tensor", "dp")),
        P("tensor", "dp"),
        P("dp"),
        P("dp"),
        P(None, "dp", "tensor"),
        P("tensor", "dp"),
        P(("dp", "tensor"), None),
    )

    return jax.shard_map(
        shards,
        mesh=mesh,
        in_specs=placed,
        out_specs=(
            P(("dp", "tensor"), None),
            P(("dp", "tensor"), None),
            P("dp"),
            P("dp"),
            P(None, "dp", "tensor"),
            P(None, ("tensor", "dp")),
            P("tensor", "dp"),
            P("dp"),
            P("dp"),
            P(None, "dp", "tensor"),
            P("tensor", "dp"),
        ),
        check_vma=False,
    )
```

```python
import functools

import jax
import jax.numpy as jnp
from jax import lax
from jax.experimental import pallas as pl
from jax.experimental.pallas import tpu as pltpu
from jax.sharding import PartitionSpec as P


HEAD_DIM = 64
ROT = 16
SEQ_LEN = 512
LANES = 128
EPS = 1e-05
F32 = jnp.float32
BF16 = jnp.bfloat16
NT = (((1,), (1,)), ((), ()))
TN = (((0,), (0,)), ((), ()))


def layer_norm(values):
    row_mean = jnp.mean(values, axis=-1, keepdims=True)
    centered = values - row_mean
    inv_sigma = lax.rsqrt(jnp.mean(centered * centered, axis=-1, keepdims=True) + EPS)
    return (centered * inv_sigma, inv_sigma)


def norm_back(grad_hat, normed, inv_sigma):
    return inv_sigma * (
        grad_hat
        - jnp.mean(grad_hat, axis=-1, keepdims=True)
        - normed * jnp.mean(grad_hat * normed, axis=-1, keepdims=True)
    )


def rotary_lanes():
    half = ROT // 2
    frequency = 10000.0 ** (-(2.0 * jnp.arange(half, dtype=F32)) / ROT)
    angles = jnp.arange(SEQ_LEN, dtype=F32)[:, None] * frequency[None, :]
    cosine, sine = jnp.cos(angles), jnp.sin(angles)
    rest = HEAD_DIM - ROT
    zero = jnp.zeros((SEQ_LEN, half), F32)
    tail = jnp.zeros((SEQ_LEN, rest), F32)
    copies = LANES // HEAD_DIM
    keep = jnp.concatenate([cosine, cosine, tail + 1.0] * copies, axis=1)
    low = jnp.concatenate([-sine, zero, tail] * copies, axis=1)
    high = jnp.concatenate([zero, sine, tail] * copies, axis=1)
    return keep, low, high


def bits_of(axis):
    size = lax.axis_size(axis)
    return [1 << b for b in range(size.bit_length() - 1)]


def swap(value, axis, bit):
    return lax.ppermute(value, axis, [(i, i ^ bit) for i in range(lax.axis_size(axis))])


def total_over(value, axis):
    for bit in bits_of(axis):
        value = value + swap(value, axis, bit)
    return value


def row_parts(rows, count):
    tiles = rows // 16
    edges = [16 * (tiles * k // count) for k in range(count)] + [rows]
    return list(zip(edges[:-1], edges[1:]))


def part_plan(rows):
    bits = bits_of("tensor")
    return [
        (lo, hi, bits[k:] + bits[:k]) for k, (lo, hi) in enumerate(row_parts(rows, len(bits)))
    ]


def together(values):
    return list(lax.optimization_barrier(tuple(values)))


def collect_rows(block):
    plan = part_plan(block.shape[0])
    held = [block[lo:hi] for lo, hi, _ in plan]
    for j in range(len(plan)):
        got = []
        for h, (_, _, order) in zip(held, plan):
            got.append(swap(h, "tensor", order[j]))
        held = together(jnp.concatenate([h, g], axis=0) for h, g in zip(held, got))
    return jnp.concatenate(held, axis=0)


def part_slices(rows):
    count = lax.axis_size("tensor")
    return [slice(lo * count, hi * count) for lo, hi, _ in part_plan(rows)]


def spread_rows(terms, rows):
    plan = part_plan(rows)
    held = list(terms)
    for j in reversed(range(len(plan))):
        totals = []
        for h, (_, _, order) in zip(held, plan):
            half = h.shape[0] // 2
            got = swap(h[half:], "tensor", order[j])
            total = h[:half].astype(F32) + got.astype(F32)
            totals.append(total.astype(BF16) if j else total)
        held = together(totals)
    return jnp.concatenate(held, axis=0)


def frame_pieces(rows):
    count = lax.axis_size("tensor")
    per_seq = SEQ_LEN // rows
    return [
        (member, lo, hi, order)
        for member in range(count)
        for lo, hi, order in part_plan(rows)
    ], per_seq * len(part_plan(rows))


def frame_offsets(rows):
    count = lax.axis_size("tensor")
    here = lax.axis_index("tensor").astype(jnp.int32)
    places = []
    for member, lo, hi, order in frame_pieces(rows)[0]:
        other = here ^ member
        place = jnp.int32(0)
        for j, bit in enumerate(order):
            place = place + jnp.where((other & bit) != 0, 1 << j, 0)
        places.append(lo * count + place * (hi - lo))
    return jnp.stack(places).astype(jnp.int32)


def ring_step(value):
    count = lax.axis_size("dp")
    return lax.ppermute(value, "dp", [(i, (i + 2) % count) for i in range(count)])


def ring_owners():
    count = lax.axis_size("dp")
    here = lax.axis_index("dp")
    return [(here - 2 * k) % count for k in range(count // 2)]


def ring_gather(shard):
    count = lax.axis_size("dp")
    size = shard.shape[0]
    full = jnp.zeros((size * count,) + shard.shape[1:], shard.dtype)
    held = shard
    for k, owner in enumerate(ring_owners()):
        if k:
            held = ring_step(held)
        full = lax.dynamic_update_slice_in_dim(full, held, owner * size, 0)
        full = lax.dynamic_update_slice_in_dim(full, swap(held, "dp", 1), (owner ^ 1) * size, 0)
    return full


def ring_reduce(grad):
    size = grad.shape[1] // lax.axis_size("dp")
    owners = ring_owners()

    def columns(owner):
        return lax.dynamic_slice_in_dim(grad, owner * size, size, 1)

    other = swap(jnp.stack([columns(owner ^ 1) for owner in owners]), "dp", 1)

    def block(k):
        return columns(owners[k]).astype(F32) + other[k].astype(F32)

    total = block(1)
    for k in list(range(2, len(owners))) + [0]:
        total = block(k) + ring_step(total.astype(BF16)).astype(F32)
    return total


def after(value, *others):
    return lax.optimization_barrier((value,) + others)[0]


def ordered(ref, lead, offs_ref, runs):
    return jnp.concatenate(
        [
            ref[lead + (pl.ds(pl.multiple_of(offs_ref[i], 16), size), slice(None))]
            for i, size in runs
        ],
        axis=0,
    )


def put_ordered(ref, lead, offs_ref, runs, value):
    at = 0
    for i, size in runs:
        ref[lead + (pl.ds(pl.multiple_of(offs_ref[i], 16), size), slice(None))] = value[
            at : at + size
        ]
        at += size


CHUNK = 256
HEADS_STEP = LANES // HEAD_DIM


def lane_roll(value, shift):
    return pltpu.roll(value, shift % LANES, 1)


def masked(scores, start):
    own = scores[:, start:]
    rows = lax.broadcasted_iota(jnp.int32, own.shape, 0)
    cols = lax.broadcasted_iota(jnp.int32, own.shape, 1)
    own = jnp.where(rows >= cols, own, -jnp.inf)
    return jnp.concatenate([scores[:, :start], own], axis=1) if start else own


def attend_kernel(offs_ref, pre_ref, keep_ref, low_ref, high_ref, qkv_ref, ctx_ref, lse_ref, *, runs):
    for seq, seq_runs in enumerate(runs):
        attend_seq(
            offs_ref, pre_ref, keep_ref, low_ref, high_ref, qkv_ref, ctx_ref, lse_ref, seq, seq_runs
        )


def attend_seq(
    offs_ref, pre_ref, keep_ref, low_ref, high_ref, qkv_ref, ctx_ref, lse_ref, seq, runs
):
    half = ROT // 2
    scale = HEAD_DIM ** (-0.5)
    keep, low, high = keep_ref[...], low_ref[...], high_ref[...]
    for c in range(3):
        v = ordered(pre_ref, (c,), offs_ref, runs)
        if c < 2:
            v = v * keep + lane_roll(v, -half) * low + lane_roll(v, half) * high
        qkv_ref[c, seq] = v.astype(BF16)
    ctx_parts, lse_parts = [], []
    for start in range(0, SEQ_LEN, CHUNK):
        end = start + CHUNK
        ctxs, lses = [], []
        for h in range(HEADS_STEP):
            cols = slice(h * HEAD_DIM, (h + 1) * HEAD_DIM)
            q = qkv_ref[0, seq, start:end, cols]
            k = qkv_ref[1, seq, :end, cols]
            v = qkv_ref[2, seq, :end, cols]
            s = lax.dot_general(q * scale, k, NT, preferred_element_type=F32)
            s = masked(s, start)
            top = jnp.max(s, axis=-1, keepdims=True)
            e = jnp.exp(s - top)
            total = jnp.sum(e, axis=-1, keepdims=True)
            p = (e * (1.0 / total)).astype(BF16)
            ctxs.append(jnp.dot(p, v, preferred_element_type=F32).astype(BF16))
            lses.append(jnp.broadcast_to(top + jnp.log(total), (CHUNK, HEAD_DIM)))
        ctx_parts.append(jnp.concatenate(ctxs, axis=1))
        lse_parts.append(jnp.concatenate(lses, axis=1))
    put_ordered(ctx_ref, (), offs_ref, runs, jnp.concatenate(ctx_parts, axis=0))
    lse_ref[seq] = jnp.concatenate(lse_parts, axis=0)


def attend_back_kernel(offs_ref, *refs, runs):
    for seq, seq_runs in enumerate(runs):
        attend_back_seq(offs_ref, *refs, seq, seq_runs)


def attend_back_seq(
    offs_ref,
    qkv_ref,
    ctx_ref,
    gctx_ref,
    lse_ref,
    keep_ref,
    low_ref,
    high_ref,
    gpre_ref,
    bias_ref,
    seq,
    runs,
):
    half = ROT // 2
    scale = HEAD_DIM ** (-0.5)
    ctx = ordered(ctx_ref, (), offs_ref, runs)
    gctx = ordered(gctx_ref, (), offs_ref, runs)
    prod = gctx.astype(F32) * ctx.astype(F32)
    starts = list(range(0, SEQ_LEN, CHUNK))
    gq, gk, gv = [], [], []
    for h in range(HEADS_STEP):
        cols = slice(h * HEAD_DIM, (h + 1) * HEAD_DIM)
        dq_parts = []
        dk = [None] * len(starts)
        dv = [None] * len(starts)
        for i, start in enumerate(starts):
            end = start + CHUNK
            q = qkv_ref[0, seq, start:end, cols]
            k = qkv_ref[1, seq, :end, cols]
            v = qkv_ref[2, seq, :end, cols]
            g = gctx[start:end, cols]
            lse = lse_ref[seq, start:end, h * HEAD_DIM : h * HEAD_DIM + 1]
            delta = jnp.sum(prod[start:end, cols], axis=-1, keepdims=True)
            s = lax.dot_general(q * scale, k, NT, preferred_element_type=F32)
            p = jnp.exp(masked(s, start) - lse)
            dp = lax.dot_general(g, v, NT, preferred_element_type=F32)
            ds = (p * (dp - delta)).astype(BF16)
            p_low = p.astype(BF16)
            dq_parts.append(jnp.dot(ds, k, preferred_element_type=F32))
            dk_i = lax.dot_general(ds, q, TN, preferred_element_type=F32)
            dv_i = lax.dot_general(p_low, g, TN, preferred_element_type=F32)
            for j in range(i + 1):
                part = slice(j * CHUNK, (j + 1) * CHUNK)
                dk[j] = dk_i[part] if dk[j] is None else dk[j] + dk_i[part]
                dv[j] = dv_i[part] if dv[j] is None else dv[j] + dv_i[part]
        gq.append(jnp.concatenate(dq_parts, axis=0) * scale)
        gk.append(jnp.concatenate(dk, axis=0) * scale)
        gv.append(jnp.concatenate(dv, axis=0))
    keep, low, high = keep_ref[...], low_ref[...], high_ref[...]
    for c, parts in enumerate((gq, gk, gv)):
        v = jnp.concatenate(parts, axis=1)
        if c < 2:
            v = v * keep - lane_roll(v, -half) * low - lane_roll(v, half) * high
        v = v.astype(BF16)
        put_ordered(gpre_ref, (c,), offs_ref, runs, v)
        bias_ref[seq, c : c + 1] = jnp.sum(v.astype(F32), axis=0, keepdims=True)


def attend_specs(seqs, group_rows):
    table = pl.BlockSpec((SEQ_LEN, LANES), lambda h, f: (0, 0))
    framed3 = pl.BlockSpec((3, group_rows, LANES), lambda h, f: (0, 0, h))
    framed = pl.BlockSpec((group_rows, LANES), lambda h, f: (0, h))
    natural3 = pl.BlockSpec((3, seqs, SEQ_LEN, LANES), lambda h, f: (0, 0, 0, h))
    natural = pl.BlockSpec((seqs, SEQ_LEN, LANES), lambda h, f: (0, 0, h))
    bias = pl.BlockSpec((seqs, 3, LANES), lambda h, f: (0, 0, h))
    return table, framed3, framed, natural3, natural, bias


def sequence_runs(rows):
    pieces, per_seq = frame_pieces(rows)
    runs = [(i, hi - lo) for i, (_, lo, hi, _) in enumerate(pieces)]
    return tuple(tuple(runs[i : i + per_seq]) for i in range(0, len(runs), per_seq))


def attend(offs, pre, tables, runs):
    _, group_rows, cols = pre.shape
    seqs = group_rows // SEQ_LEN
    table, framed3, framed, natural3, natural, _ = attend_specs(seqs, group_rows)
    return pl.pallas_call(
        functools.partial(attend_kernel, runs=runs),
        out_shape=(
            jax.ShapeDtypeStruct((3, seqs, SEQ_LEN, cols), BF16),
            jax.ShapeDtypeStruct((group_rows, cols), BF16),
            jax.ShapeDtypeStruct((seqs, SEQ_LEN, cols), F32),
        ),
        grid_spec=pltpu.PrefetchScalarGridSpec(
            num_scalar_prefetch=1,
            grid=(cols // LANES,),
            in_specs=[framed3, table, table, table],
            out_specs=[natural3, framed, natural],
        ),
        name="attend",
    )(offs, pre, *tables)


def attend_back(offs, qkv, ctx, gctx, lse, tables, runs):
    _, seqs, _, cols = qkv.shape
    group_rows = seqs * SEQ_LEN
    table, framed3, framed, natural3, natural, bias = attend_specs(seqs, group_rows)
    return pl.pallas_call(
        functools.partial(attend_back_kernel, runs=runs),
        out_shape=(
            jax.ShapeDtypeStruct((3, group_rows, cols), BF16),
            jax.ShapeDtypeStruct((seqs, 3, cols), F32),
        ),
        grid_spec=pltpu.PrefetchScalarGridSpec(
            num_scalar_prefetch=1,
            grid=(cols // LANES,),
            in_specs=[natural3, framed, framed, natural, table, table, table],
            out_specs=[framed3, bias],
        ),
        name="attend_back",
    )(offs, qkv, ctx, gctx, lse, *tables)


def shards(
    layer_input,
    norm1_gain,
    norm1_bias,
    qkv_weight,
    qkv_bias,
    out_weight,
    norm2_gain,
    norm2_bias,
    gate_up_weight,
    down_weight,
    out_cotangent,
):
    rows, width = layer_input.shape
    part = norm1_gain.shape[0]
    dp_count = lax.axis_size("dp")
    dp_here = lax.axis_index("dp")
    head_cols = qkv_weight.shape[2]
    offs = frame_offsets(rows)
    runs = sequence_runs(rows)
    tables = rotary_lanes()

    qkv_local = lax.all_gather(qkv_weight, "dp", axis=1, tiled=True)
    gate_up_local = lax.all_gather(gate_up_weight, "dp", axis=1, tiled=True)
    down_local = lax.all_gather(down_weight, "dp", axis=1, tiled=True)

    packed = jnp.concatenate(
        [norm1_gain, norm1_bias, norm2_gain, norm2_bias, qkv_bias.reshape(-1)]
    )
    packed = lax.all_gather(packed, "dp", axis=0, tiled=False)
    x_rows = collect_rows(layer_input)
    cot_rows = collect_rows(after(out_cotangent, x_rows))
    gain_one, bias_one, gain_two, bias_two = (
        packed[:, k * part : (k + 1) * part].reshape(width).astype(F32) for k in range(4)
    )
    bias_local = (
        packed[:, 4 * part :].reshape(dp_count, 3, -1).transpose(1, 0, 2).reshape(3, head_cols)
    ).astype(F32)

    x_float = layer_input.astype(F32)
    hat_one, inv_one = layer_norm(x_float)
    out_turned = ring_gather(out_weight.T)
    rows_one = (layer_norm(x_rows.astype(F32))[0] * gain_one + bias_one).astype(BF16)
    pre = (
        jnp.einsum("rd,cdk->crk", rows_one, qkv_local, preferred_element_type=F32)
        + bias_local[:, None, :]
    )
    qkv_heads, context, lse = attend(offs, pre, tables, runs)
    parts = part_slices(rows)
    attn_terms = [
        lax.dot_general(context[at], out_turned, NT, preferred_element_type=F32).astype(BF16)
        for at in parts
    ]
    residual = x_float + spread_rows(attn_terms, rows)

    hat_two, inv_two = layer_norm(residual)
    rows_two = collect_rows((hat_two * gain_two + bias_two).astype(BF16))
    gate_proj = jnp.dot(rows_two, gate_up_local[0], preferred_element_type=F32)
    up_proj = jnp.dot(rows_two, gate_up_local[1], preferred_element_type=F32)
    sigmoid_gate = jax.nn.sigmoid(gate_proj)
    silu_gate = gate_proj * sigmoid_gate
    activation = (silu_gate * up_proj).astype(BF16)

    grad_down = lax.dot_general(
        activation, cot_rows, TN, preferred_element_type=F32
    ).astype(BF16)
    share_down = lax.psum_scatter(grad_down, "dp", scatter_dimension=1, tiled=True)
    share_down = share_down.astype(F32)
    grad_act = lax.dot_general(
        after(cot_rows, grad_down), down_local, NT, preferred_element_type=F32
    )
    grad_gate = (
        grad_act * up_proj * sigmoid_gate * (1.0 + gate_proj * (1.0 - sigmoid_gate))
    ).astype(BF16)
    grad_up = (grad_act * silu_gate).astype(BF16)
    back_terms = [
        (
            lax.dot_general(grad_gate[at], gate_up_local[0], NT, preferred_element_type=F32)
            + lax.dot_general(grad_up[at], gate_up_local[1], NT, preferred_element_type=F32)
        ).astype(BF16)
        for at in parts
    ]
    grad_normed_two = spread_rows(back_terms, rows)
    grad_gate_up = jnp.stack([grad_gate, grad_up])
    grad_wgate_up = jnp.einsum(
        "rd,crk->cdk",
        after(rows_two, *back_terms),
        grad_gate_up,
        preferred_element_type=F32,
    ).astype(BF16)
    share_gate_up = lax.psum_scatter(grad_wgate_up, "dp", scatter_dimension=1, tiled=True)
    share_gate_up = share_gate_up.astype(F32)
    grad_normed_two, _, mlp_act = lax.optimization_barrier(
        (grad_normed_two, grad_wgate_up, activation)
    )
    grad_resid = out_cotangent.astype(F32) + norm_back(
        grad_normed_two * gain_two, hat_two, inv_two
    )

    mlp_terms = jnp.dot(mlp_act, down_local, preferred_element_type=F32).astype(BF16)
    resid_rows, mlp_terms = lax.optimization_barrier(
        (collect_rows(grad_resid.astype(BF16)), mlp_terms)
    )
    grad_context = jnp.dot(resid_rows, out_turned, preferred_element_type=F32).astype(BF16)
    grad_pre, bias_sums = attend_back(offs, qkv_heads, context, grad_context, lse, tables, runs)
    grad_wqkv = jnp.einsum(
        "rd,crk->cdk", rows_one, grad_pre, preferred_element_type=F32
    ).astype(BF16)
    share_qkv = lax.psum_scatter(grad_wqkv, "dp", scatter_dimension=1, tiled=True)
    share_qkv = share_qkv.astype(F32)
    late_pre = after(grad_pre, grad_wqkv)
    qkv_terms = [
        jnp.einsum(
            "crk,cdk->rd", late_pre[:, at], qkv_local, preferred_element_type=F32
        ).astype(BF16)
        for at in parts
    ]
    grad_normed_one = spread_rows(qkv_terms, rows)
    grad_wout = lax.dot_general(
        after(context, *qkv_terms), resid_rows, TN, preferred_element_type=F32
    ).astype(BF16)
    share_out = ring_reduce(grad_wout)
    grad_input = grad_resid + norm_back(grad_normed_one * gain_one, hat_one, inv_one)
    mlp_terms = after(mlp_terms, grad_normed_one)
    layer_output = (residual + spread_rows([mlp_terms[at] for at in parts], rows)).astype(BF16)

    norm_sums = jnp.stack(
        [
            jnp.sum(grad_normed_one * hat_one, axis=0),
            jnp.sum(grad_normed_one, axis=0),
            jnp.sum(grad_normed_two * hat_two, axis=0),
            jnp.sum(grad_normed_two, axis=0),
        ]
    )
    norm_total = total_over(norm_sums, "tensor").reshape(-1)
    bias_total = jnp.sum(bias_sums, axis=0).reshape(-1)
    totals = total_over(jnp.concatenate([norm_total, bias_total]), "dp")
    norm_total = totals[: 4 * width].reshape(4, width)
    bias_total = totals[4 * width :].reshape(3, head_cols)
    share_norm = lax.dynamic_slice_in_dim(norm_total, dp_here * part, part, axis=1)
    bias_part = qkv_bias.shape[1]
    share_bias = lax.dynamic_slice_in_dim(bias_total, dp_here * bias_part, bias_part, axis=1)
    return (
        layer_output,
        grad_input,
        share_norm[0],
        share_norm[1],
        share_qkv,
        share_bias,
        share_out,
        share_norm[2],
        share_norm[3],
        share_gate_up,
        share_down,
    )


def solution(mesh):
    placed = (
        P(("dp", "tensor"), None),
        P("dp"),
        P("dp"),
        P(None, "dp", "tensor"),
        P(None, ("tensor", "dp")),
        P("tensor", "dp"),
        P("dp"),
        P("dp"),
        P(None, "dp", "tensor"),
        P("tensor", "dp"),
        P(("dp", "tensor"), None),
    )

    return jax.shard_map(
        shards,
        mesh=mesh,
        in_specs=placed,
        out_specs=(
            P(("dp", "tensor"), None),
            P(("dp", "tensor"), None),
            P("dp"),
            P("dp"),
            P(None, "dp", "tensor"),
            P(None, ("tensor", "dp")),
            P("tensor", "dp"),
            P("dp"),
            P("dp"),
            P(None, "dp", "tensor"),
            P("tensor", "dp"),
        ),
        check_vma=False,
    )
```

```python
import functools

import jax
import jax.numpy as jnp
from jax import lax
from jax.experimental import pallas as pl
from jax.experimental.pallas import tpu as pltpu
from jax.sharding import PartitionSpec as P


HEAD_DIM = 64
ROT = 16
SEQ_LEN = 512
LANES = 128
EPS = 1e-05
F32 = jnp.float32
BF16 = jnp.bfloat16
NT = (((1,), (1,)), ((), ()))
TN = (((0,), (0,)), ((), ()))


def layer_norm(values):
    row_mean = jnp.mean(values, axis=-1, keepdims=True)
    centered = values - row_mean
    inv_sigma = lax.rsqrt(jnp.mean(centered * centered, axis=-1, keepdims=True) + EPS)
    return (centered * inv_sigma, inv_sigma)


def norm_back(grad_hat, normed, inv_sigma):
    return inv_sigma * (
        grad_hat
        - jnp.mean(grad_hat, axis=-1, keepdims=True)
        - normed * jnp.mean(grad_hat * normed, axis=-1, keepdims=True)
    )


def rotary_lanes():
    half = ROT // 2
    frequency = 10000.0 ** (-(2.0 * jnp.arange(half, dtype=F32)) / ROT)
    angles = jnp.arange(SEQ_LEN, dtype=F32)[:, None] * frequency[None, :]
    cosine, sine = jnp.cos(angles), jnp.sin(angles)
    rest = HEAD_DIM - ROT
    zero = jnp.zeros((SEQ_LEN, half), F32)
    tail = jnp.zeros((SEQ_LEN, rest), F32)
    copies = LANES // HEAD_DIM
    keep = jnp.concatenate([cosine, cosine, tail + 1.0] * copies, axis=1)
    low = jnp.concatenate([-sine, zero, tail] * copies, axis=1)
    high = jnp.concatenate([zero, sine, tail] * copies, axis=1)
    return keep, low, high


def bits_of(axis):
    size = lax.axis_size(axis)
    return [1 << b for b in range(size.bit_length() - 1)]


def swap(value, axis, bit):
    return lax.ppermute(value, axis, [(i, i ^ bit) for i in range(lax.axis_size(axis))])


def total_over(value, axis):
    for bit in bits_of(axis):
        value = value + swap(value, axis, bit)
    return value


def row_parts(rows, count):
    tiles = rows // 16
    edges = [16 * (tiles * k // count) for k in range(count)] + [rows]
    return list(zip(edges[:-1], edges[1:]))


def part_plan(rows):
    bits = bits_of("tensor")
    return [
        (lo, hi, bits[k:] + bits[:k]) for k, (lo, hi) in enumerate(row_parts(rows, len(bits)))
    ]


def together(values):
    return list(lax.optimization_barrier(tuple(values)))


def collect_rows(block):
    plan = part_plan(block.shape[0])
    held = [block[lo:hi] for lo, hi, _ in plan]
    for j in range(len(plan)):
        got = []
        for h, (_, _, order) in zip(held, plan):
            got.append(swap(h, "tensor", order[j]))
        held = together(jnp.concatenate([h, g], axis=0) for h, g in zip(held, got))
    return jnp.concatenate(held, axis=0)


def part_slices(rows):
    count = lax.axis_size("tensor")
    return [slice(lo * count, hi * count) for lo, hi, _ in part_plan(rows)]


def spread_rows(terms, rows):
    plan = part_plan(rows)
    held = list(terms)
    for j in reversed(range(len(plan))):
        totals = []
        for h, (_, _, order) in zip(held, plan):
            half = h.shape[0] // 2
            got = swap(h[half:], "tensor", order[j])
            total = h[:half].astype(F32) + got.astype(F32)
            totals.append(total.astype(BF16) if j else total)
        held = together(totals)
    return jnp.concatenate(held, axis=0)


def frame_pieces(rows):
    count = lax.axis_size("tensor")
    per_seq = SEQ_LEN // rows
    return [
        (member, lo, hi, order)
        for member in range(count)
        for lo, hi, order in part_plan(rows)
    ], per_seq * len(part_plan(rows))


def frame_offsets(rows):
    count = lax.axis_size("tensor")
    here = lax.axis_index("tensor").astype(jnp.int32)
    places = []
    for member, lo, hi, order in frame_pieces(rows)[0]:
        other = here ^ member
        place = jnp.int32(0)
        for j, bit in enumerate(order):
            place = place + jnp.where((other & bit) != 0, 1 << j, 0)
        places.append(lo * count + place * (hi - lo))
    return jnp.stack(places).astype(jnp.int32)


def ring_step(value):
    count = lax.axis_size("dp")
    return lax.ppermute(value, "dp", [(i, (i + 2) % count) for i in range(count)])


def ring_owners():
    count = lax.axis_size("dp")
    here = lax.axis_index("dp")
    return [(here - 2 * k) % count for k in range(count // 2)]


def ring_gather(shard):
    count = lax.axis_size("dp")
    size = shard.shape[0]
    full = jnp.zeros((size * count,) + shard.shape[1:], shard.dtype)
    held = shard
    for k, owner in enumerate(ring_owners()):
        if k:
            held = ring_step(held)
        full = lax.dynamic_update_slice_in_dim(full, held, owner * size, 0)
        full = lax.dynamic_update_slice_in_dim(full, swap(held, "dp", 1), (owner ^ 1) * size, 0)
    return full


def ring_reduce(grad):
    size = grad.shape[1] // lax.axis_size("dp")
    owners = ring_owners()

    def columns(owner):
        return lax.dynamic_slice_in_dim(grad, owner * size, size, 1)

    other = swap(jnp.stack([columns(owner ^ 1) for owner in owners]), "dp", 1)

    def block(k):
        return columns(owners[k]).astype(F32) + other[k].astype(F32)

    total = block(1)
    for k in list(range(2, len(owners))) + [0]:
        total = block(k) + ring_step(total.astype(BF16)).astype(F32)
    return total


def core_halves(grad):
    count = lax.axis_size("dp")
    size = grad.shape[1] // count
    core = lax.axis_index("dp") % 2

    def half(which):
        return jnp.concatenate(
            [
                lax.dynamic_slice_in_dim(grad, (2 * z + which) * size, size, 1)
                for z in range(count // 2)
            ],
            axis=1,
        )

    got = swap(half(1 - core), "dp", 1)
    return (half(core).astype(F32) + got.astype(F32)).astype(BF16)


def after(value, *others):
    return lax.optimization_barrier((value,) + others)[0]


def ordered(ref, lead, offs_ref, runs):
    return jnp.concatenate(
        [
            ref[lead + (pl.ds(pl.multiple_of(offs_ref[i], 16), size), slice(None))]
            for i, size in runs
        ],
        axis=0,
    )


def put_ordered(ref, lead, offs_ref, runs, value):
    at = 0
    for i, size in runs:
        ref[lead + (pl.ds(pl.multiple_of(offs_ref[i], 16), size), slice(None))] = value[
            at : at + size
        ]
        at += size


CHUNK = 256
HEADS_STEP = LANES // HEAD_DIM


def lane_roll(value, shift):
    return pltpu.roll(value, shift % LANES, 1)


def masked(scores, start):
    own = scores[:, start:]
    rows = lax.broadcasted_iota(jnp.int32, own.shape, 0)
    cols = lax.broadcasted_iota(jnp.int32, own.shape, 1)
    own = jnp.where(rows >= cols, own, -jnp.inf)
    return jnp.concatenate([scores[:, :start], own], axis=1) if start else own


def attend_kernel(offs_ref, pre_ref, keep_ref, low_ref, high_ref, qkv_ref, ctx_ref, lse_ref, *, runs):
    for seq, seq_runs in enumerate(runs):
        attend_seq(
            offs_ref, pre_ref, keep_ref, low_ref, high_ref, qkv_ref, ctx_ref, lse_ref, seq, seq_runs
        )


def attend_seq(
    offs_ref, pre_ref, keep_ref, low_ref, high_ref, qkv_ref, ctx_ref, lse_ref, seq, runs
):
    half = ROT // 2
    scale = HEAD_DIM ** (-0.5)
    keep, low, high = keep_ref[...], low_ref[...], high_ref[...]
    for c in range(3):
        v = ordered(pre_ref, (c,), offs_ref, runs)
        if c < 2:
            v = v * keep + lane_roll(v, -half) * low + lane_roll(v, half) * high
        qkv_ref[c, seq] = v.astype(BF16)
    ctx_parts, lse_parts = [], []
    for start in range(0, SEQ_LEN, CHUNK):
        end = start + CHUNK
        ctxs, lses = [], []
        for h in range(HEADS_STEP):
            cols = slice(h * HEAD_DIM, (h + 1) * HEAD_DIM)
            q = qkv_ref[0, seq, start:end, cols]
            k = qkv_ref[1, seq, :end, cols]
            v = qkv_ref[2, seq, :end, cols]
            s = lax.dot_general(q * scale, k, NT, preferred_element_type=F32)
            s = masked(s, start)
            top = jnp.max(s, axis=-1, keepdims=True)
            e = jnp.exp(s - top)
            total = jnp.sum(e, axis=-1, keepdims=True)
            p = (e * (1.0 / total)).astype(BF16)
            ctxs.append(jnp.dot(p, v, preferred_element_type=F32).astype(BF16))
            lses.append(jnp.broadcast_to(top + jnp.log(total), (CHUNK, HEAD_DIM)))
        ctx_parts.append(jnp.concatenate(ctxs, axis=1))
        lse_parts.append(jnp.concatenate(lses, axis=1))
    put_ordered(ctx_ref, (), offs_ref, runs, jnp.concatenate(ctx_parts, axis=0))
    lse_ref[seq] = jnp.concatenate(lse_parts, axis=0)


def attend_back_kernel(offs_ref, *refs, runs):
    for seq, seq_runs in enumerate(runs):
        attend_back_seq(offs_ref, *refs, seq, seq_runs)


def attend_back_seq(
    offs_ref,
    qkv_ref,
    ctx_ref,
    gctx_ref,
    lse_ref,
    keep_ref,
    low_ref,
    high_ref,
    gpre_ref,
    bias_ref,
    seq,
    runs,
):
    half = ROT // 2
    scale = HEAD_DIM ** (-0.5)
    ctx = ordered(ctx_ref, (), offs_ref, runs)
    gctx = ordered(gctx_ref, (), offs_ref, runs)
    prod = gctx.astype(F32) * ctx.astype(F32)
    starts = list(range(0, SEQ_LEN, CHUNK))
    gq, gk, gv = [], [], []
    for h in range(HEADS_STEP):
        cols = slice(h * HEAD_DIM, (h + 1) * HEAD_DIM)
        dq_parts = []
        dk = [None] * len(starts)
        dv = [None] * len(starts)
        for i, start in enumerate(starts):
            end = start + CHUNK
            q = qkv_ref[0, seq, start:end, cols]
            k = qkv_ref[1, seq, :end, cols]
            v = qkv_ref[2, seq, :end, cols]
            g = gctx[start:end, cols]
            lse = lse_ref[seq, start:end, h * HEAD_DIM : h * HEAD_DIM + 1]
            delta = jnp.sum(prod[start:end, cols], axis=-1, keepdims=True)
            s = lax.dot_general(q * scale, k, NT, preferred_element_type=F32)
            p = jnp.exp(masked(s, start) - lse)
            dp = lax.dot_general(g, v, NT, preferred_element_type=F32)
            ds = (p * (dp - delta)).astype(BF16)
            p_low = p.astype(BF16)
            dq_parts.append(jnp.dot(ds, k, preferred_element_type=F32))
            dk_i = lax.dot_general(ds, q, TN, preferred_element_type=F32)
            dv_i = lax.dot_general(p_low, g, TN, preferred_element_type=F32)
            for j in range(i + 1):
                part = slice(j * CHUNK, (j + 1) * CHUNK)
                dk[j] = dk_i[part] if dk[j] is None else dk[j] + dk_i[part]
                dv[j] = dv_i[part] if dv[j] is None else dv[j] + dv_i[part]
        gq.append(jnp.concatenate(dq_parts, axis=0) * scale)
        gk.append(jnp.concatenate(dk, axis=0) * scale)
        gv.append(jnp.concatenate(dv, axis=0))
    keep, low, high = keep_ref[...], low_ref[...], high_ref[...]
    for c, parts in enumerate((gq, gk, gv)):
        v = jnp.concatenate(parts, axis=1)
        if c < 2:
            v = v * keep - lane_roll(v, -half) * low - lane_roll(v, half) * high
        v = v.astype(BF16)
        put_ordered(gpre_ref, (c,), offs_ref, runs, v)
        bias_ref[seq, c : c + 1] = jnp.sum(v.astype(F32), axis=0, keepdims=True)


def attend_specs(seqs, group_rows):
    table = pl.BlockSpec((SEQ_LEN, LANES), lambda h, f: (0, 0))
    framed3 = pl.BlockSpec((3, group_rows, LANES), lambda h, f: (0, 0, h))
    framed = pl.BlockSpec((group_rows, LANES), lambda h, f: (0, h))
    natural3 = pl.BlockSpec((3, seqs, SEQ_LEN, LANES), lambda h, f: (0, 0, 0, h))
    natural = pl.BlockSpec((seqs, SEQ_LEN, LANES), lambda h, f: (0, 0, h))
    bias = pl.BlockSpec((seqs, 3, LANES), lambda h, f: (0, 0, h))
    return table, framed3, framed, natural3, natural, bias


def sequence_runs(rows):
    pieces, per_seq = frame_pieces(rows)
    runs = [(i, hi - lo) for i, (_, lo, hi, _) in enumerate(pieces)]
    return tuple(tuple(runs[i : i + per_seq]) for i in range(0, len(runs), per_seq))


def attend(offs, pre, tables, runs):
    _, group_rows, cols = pre.shape
    seqs = group_rows // SEQ_LEN
    table, framed3, framed, natural3, natural, _ = attend_specs(seqs, group_rows)
    return pl.pallas_call(
        functools.partial(attend_kernel, runs=runs),
        out_shape=(
            jax.ShapeDtypeStruct((3, seqs, SEQ_LEN, cols), BF16),
            jax.ShapeDtypeStruct((group_rows, cols), BF16),
            jax.ShapeDtypeStruct((seqs, SEQ_LEN, cols), F32),
        ),
        grid_spec=pltpu.PrefetchScalarGridSpec(
            num_scalar_prefetch=1,
            grid=(cols // LANES,),
            in_specs=[framed3, table, table, table],
            out_specs=[natural3, framed, natural],
        ),
        name="attend",
    )(offs, pre, *tables)


def attend_back(offs, qkv, ctx, gctx, lse, tables, runs):
    _, seqs, _, cols = qkv.shape
    group_rows = seqs * SEQ_LEN
    table, framed3, framed, natural3, natural, bias = attend_specs(seqs, group_rows)
    return pl.pallas_call(
        functools.partial(attend_back_kernel, runs=runs),
        out_shape=(
            jax.ShapeDtypeStruct((3, group_rows, cols), BF16),
            jax.ShapeDtypeStruct((seqs, 3, cols), F32),
        ),
        grid_spec=pltpu.PrefetchScalarGridSpec(
            num_scalar_prefetch=1,
            grid=(cols // LANES,),
            in_specs=[natural3, framed, framed, natural, table, table, table],
            out_specs=[framed3, bias],
        ),
        name="attend_back",
    )(offs, qkv, ctx, gctx, lse, *tables)


def shards(
    layer_input,
    norm1_gain,
    norm1_bias,
    qkv_weight,
    qkv_bias,
    out_weight,
    norm2_gain,
    norm2_bias,
    gate_up_weight,
    down_weight,
    out_cotangent,
):
    rows, width = layer_input.shape
    part = norm1_gain.shape[0]
    dp_count = lax.axis_size("dp")
    dp_here = lax.axis_index("dp")
    head_cols = qkv_weight.shape[2]
    offs = frame_offsets(rows)
    runs = sequence_runs(rows)
    tables = rotary_lanes()

    qkv_local = lax.all_gather(qkv_weight, "dp", axis=1, tiled=True)
    gate_up_local = lax.all_gather(gate_up_weight, "dp", axis=1, tiled=True)
    down_local = lax.all_gather(down_weight, "dp", axis=1, tiled=True)

    packed = jnp.concatenate(
        [norm1_gain, norm1_bias, norm2_gain, norm2_bias, qkv_bias.reshape(-1)]
    )
    packed = lax.all_gather(packed, "dp", axis=0, tiled=False)
    x_rows = collect_rows(layer_input)
    cot_rows = collect_rows(after(out_cotangent, x_rows))
    gain_one, bias_one, gain_two, bias_two = (
        packed[:, k * part : (k + 1) * part].reshape(width).astype(F32) for k in range(4)
    )
    bias_local = (
        packed[:, 4 * part :].reshape(dp_count, 3, -1).transpose(1, 0, 2).reshape(3, head_cols)
    ).astype(F32)

    x_float = layer_input.astype(F32)
    hat_one, inv_one = layer_norm(x_float)
    out_turned = ring_gather(out_weight.T)
    rows_one = (layer_norm(x_rows.astype(F32))[0] * gain_one + bias_one).astype(BF16)
    pre = (
        jnp.einsum("rd,cdk->crk", rows_one, qkv_local, preferred_element_type=F32)
        + bias_local[:, None, :]
    )
    qkv_heads, context, lse = attend(offs, pre, tables, runs)
    parts = part_slices(rows)
    attn_terms = [
        lax.dot_general(context[at], out_turned, NT, preferred_element_type=F32).astype(BF16)
        for at in parts
    ]
    residual = x_float + spread_rows(attn_terms, rows)

    hat_two, inv_two = layer_norm(residual)
    rows_two = collect_rows((hat_two * gain_two + bias_two).astype(BF16))
    gate_proj = jnp.dot(rows_two, gate_up_local[0], preferred_element_type=F32)
    up_proj = jnp.dot(rows_two, gate_up_local[1], preferred_element_type=F32)
    sigmoid_gate = jax.nn.sigmoid(gate_proj)
    silu_gate = gate_proj * sigmoid_gate
    activation = (silu_gate * up_proj).astype(BF16)

    grad_down = lax.dot_general(
        activation, cot_rows, TN, preferred_element_type=F32
    ).astype(BF16)
    share_down = lax.psum_scatter(grad_down, "dp", scatter_dimension=1, tiled=True)
    share_down = share_down.astype(F32)
    grad_act = lax.dot_general(
        after(cot_rows, grad_down), down_local, NT, preferred_element_type=F32
    )
    grad_gate = (
        grad_act * up_proj * sigmoid_gate * (1.0 + gate_proj * (1.0 - sigmoid_gate))
    ).astype(BF16)
    grad_up = (grad_act * silu_gate).astype(BF16)
    back_terms = [
        (
            lax.dot_general(grad_gate[at], gate_up_local[0], NT, preferred_element_type=F32)
            + lax.dot_general(grad_up[at], gate_up_local[1], NT, preferred_element_type=F32)
        ).astype(BF16)
        for at in parts
    ]
    grad_normed_two = spread_rows(back_terms, rows)
    grad_gate_up = jnp.stack([grad_gate, grad_up])
    grad_wgate_up = jnp.einsum(
        "rd,crk->cdk",
        after(rows_two, *back_terms),
        grad_gate_up,
        preferred_element_type=F32,
    ).astype(BF16)
    share_gate_up = lax.psum_scatter(grad_wgate_up, "dp", scatter_dimension=1, tiled=True)
    share_gate_up = share_gate_up.astype(F32)
    grad_normed_two, _, mlp_act = lax.optimization_barrier(
        (grad_normed_two, grad_wgate_up, activation)
    )
    grad_resid = out_cotangent.astype(F32) + norm_back(
        grad_normed_two * gain_two, hat_two, inv_two
    )

    mlp_terms = jnp.dot(mlp_act, down_local, preferred_element_type=F32).astype(BF16)
    resid_rows, mlp_terms = lax.optimization_barrier(
        (collect_rows(grad_resid.astype(BF16)), mlp_terms)
    )
    grad_context = jnp.dot(resid_rows, out_turned, preferred_element_type=F32).astype(BF16)
    grad_pre, bias_sums = attend_back(offs, qkv_heads, context, grad_context, lse, tables, runs)
    grad_wqkv = jnp.einsum(
        "crk,rd->ckd", grad_pre, rows_one, preferred_element_type=F32
    ).astype(BF16)
    wqkv_half = core_halves(grad_wqkv.reshape(3 * head_cols, width))
    share_qkv = lax.psum_scatter(
        wqkv_half,
        "dp",
        scatter_dimension=1,
        tiled=True,
        axis_index_groups=[list(range(c, dp_count, 2)) for c in range(2)],
    )
    share_qkv = share_qkv.astype(F32).reshape(3, head_cols, part).transpose(0, 2, 1)
    layer_output = (residual + spread_rows([mlp_terms[at] for at in parts], rows)).astype(BF16)
    late_pre, layer_output = lax.optimization_barrier((grad_pre, layer_output, grad_wqkv))[:2]
    qkv_terms = [
        jnp.einsum(
            "crk,cdk->rd", late_pre[:, at], qkv_local, preferred_element_type=F32
        ).astype(BF16)
        for at in parts
    ]
    grad_normed_one = spread_rows(qkv_terms, rows)
    grad_wout = lax.dot_general(
        after(context, *qkv_terms), resid_rows, TN, preferred_element_type=F32
    ).astype(BF16)
    share_out = ring_reduce(grad_wout)
    grad_input = grad_resid + norm_back(grad_normed_one * gain_one, hat_one, inv_one)

    norm_sums = jnp.stack(
        [
            jnp.sum(grad_normed_one * hat_one, axis=0),
            jnp.sum(grad_normed_one, axis=0),
            jnp.sum(grad_normed_two * hat_two, axis=0),
            jnp.sum(grad_normed_two, axis=0),
        ]
    )
    norm_total, share_gate_up, share_down = lax.optimization_barrier(
        (total_over(norm_sums, "tensor"), share_gate_up, share_down)
    )
    norm_total = norm_total.reshape(-1)
    bias_total = jnp.sum(bias_sums, axis=0).reshape(-1)
    totals = total_over(jnp.concatenate([norm_total, bias_total]), "dp")
    norm_total = totals[: 4 * width].reshape(4, width)
    bias_total = totals[4 * width :].reshape(3, head_cols)
    share_norm = lax.dynamic_slice_in_dim(norm_total, dp_here * part, part, axis=1)
    bias_part = qkv_bias.shape[1]
    share_bias = lax.dynamic_slice_in_dim(bias_total, dp_here * bias_part, bias_part, axis=1)
    return (
        layer_output,
        grad_input,
        share_norm[0],
        share_norm[1],
        share_qkv,
        share_bias,
        share_out,
        share_norm[2],
        share_norm[3],
        share_gate_up,
        share_down,
    )


def solution(mesh):
    placed = (
        P(("dp", "tensor"), None),
        P("dp"),
        P("dp"),
        P(None, "dp", "tensor"),
        P(None, ("tensor", "dp")),
        P("tensor", "dp"),
        P("dp"),
        P("dp"),
        P(None, "dp", "tensor"),
        P("tensor", "dp"),
        P(("dp", "tensor"), None),
    )

    return jax.shard_map(
        shards,
        mesh=mesh,
        in_specs=placed,
        out_specs=(
            P(("dp", "tensor"), None),
            P(("dp", "tensor"), None),
            P("dp"),
            P("dp"),
            P(None, "dp", "tensor"),
            P(None, ("tensor", "dp")),
            P("tensor", "dp"),
            P("dp"),
            P("dp"),
            P(None, "dp", "tensor"),
            P("tensor", "dp"),
        ),
        check_vma=False,
    )
```

```python
import functools

import jax
import jax.numpy as jnp
from jax import lax
from jax.experimental import pallas as pl
from jax.experimental.pallas import tpu as pltpu
from jax.sharding import PartitionSpec as P


HEAD_DIM = 64
ROT = 16
SEQ_LEN = 512
LANES = 128
EPS = 1e-05
F32 = jnp.float32
BF16 = jnp.bfloat16
NT = (((1,), (1,)), ((), ()))
TN = (((0,), (0,)), ((), ()))


def layer_norm(values):
    row_mean = jnp.mean(values, axis=-1, keepdims=True)
    centered = values - row_mean
    inv_sigma = lax.rsqrt(jnp.mean(centered * centered, axis=-1, keepdims=True) + EPS)
    return (centered * inv_sigma, inv_sigma)


def norm_back(grad_hat, normed, inv_sigma):
    return inv_sigma * (
        grad_hat
        - jnp.mean(grad_hat, axis=-1, keepdims=True)
        - normed * jnp.mean(grad_hat * normed, axis=-1, keepdims=True)
    )


def rotary_lanes():
    half = ROT // 2
    frequency = 10000.0 ** (-(2.0 * jnp.arange(half, dtype=F32)) / ROT)
    angles = jnp.arange(SEQ_LEN, dtype=F32)[:, None] * frequency[None, :]
    cosine, sine = jnp.cos(angles), jnp.sin(angles)
    rest = HEAD_DIM - ROT
    zero = jnp.zeros((SEQ_LEN, half), F32)
    tail = jnp.zeros((SEQ_LEN, rest), F32)
    copies = LANES // HEAD_DIM
    keep = jnp.concatenate([cosine, cosine, tail + 1.0] * copies, axis=1)
    low = jnp.concatenate([-sine, zero, tail] * copies, axis=1)
    high = jnp.concatenate([zero, sine, tail] * copies, axis=1)
    return keep, low, high


def bits_of(axis):
    size = lax.axis_size(axis)
    return [1 << b for b in range(size.bit_length() - 1)]


def swap(value, axis, bit):
    return lax.ppermute(value, axis, [(i, i ^ bit) for i in range(lax.axis_size(axis))])


def total_over(value, axis):
    for bit in bits_of(axis):
        value = value + swap(value, axis, bit)
    return value


def row_parts(rows, count):
    tiles = rows // 16
    edges = [16 * (tiles * k // count) for k in range(count)] + [rows]
    return list(zip(edges[:-1], edges[1:]))


def part_plan(rows):
    bits = bits_of("tensor")
    return [
        (lo, hi, bits[k:] + bits[:k]) for k, (lo, hi) in enumerate(row_parts(rows, len(bits)))
    ]


def together(values):
    return list(lax.optimization_barrier(tuple(values)))


def collect_rows(block):
    plan = part_plan(block.shape[0])
    held = [block[lo:hi] for lo, hi, _ in plan]
    for j in range(len(plan)):
        got = []
        for h, (_, _, order) in zip(held, plan):
            got.append(swap(h, "tensor", order[j]))
        held = together(jnp.concatenate([h, g], axis=0) for h, g in zip(held, got))
    return jnp.concatenate(held, axis=0)


def part_slices(rows):
    count = lax.axis_size("tensor")
    return [slice(lo * count, hi * count) for lo, hi, _ in part_plan(rows)]


def spread_rows(terms, rows):
    plan = part_plan(rows)
    held = list(terms)
    for j in reversed(range(len(plan))):
        totals = []
        for h, (_, _, order) in zip(held, plan):
            half = h.shape[0] // 2
            got = swap(h[half:], "tensor", order[j])
            total = h[:half].astype(F32) + got.astype(F32)
            totals.append(total.astype(BF16) if j else total)
        held = together(totals)
    return jnp.concatenate(held, axis=0)


def frame_pieces(rows):
    count = lax.axis_size("tensor")
    per_seq = SEQ_LEN // rows
    return [
        (member, lo, hi, order)
        for member in range(count)
        for lo, hi, order in part_plan(rows)
    ], per_seq * len(part_plan(rows))


def frame_offsets(rows):
    count = lax.axis_size("tensor")
    here = lax.axis_index("tensor").astype(jnp.int32)
    places = []
    for member, lo, hi, order in frame_pieces(rows)[0]:
        other = here ^ member
        place = jnp.int32(0)
        for j, bit in enumerate(order):
            place = place + jnp.where((other & bit) != 0, 1 << j, 0)
        places.append(lo * count + place * (hi - lo))
    return jnp.stack(places).astype(jnp.int32)


def ring_step(value):
    count = lax.axis_size("dp")
    return lax.ppermute(value, "dp", [(i, (i + 2) % count) for i in range(count)])


def ring_owners():
    count = lax.axis_size("dp")
    here = lax.axis_index("dp")
    return [(here - 2 * k) % count for k in range(count // 2)]


def ring_gather(shard):
    count = lax.axis_size("dp")
    size = shard.shape[0]
    full = jnp.zeros((size * count,) + shard.shape[1:], shard.dtype)
    held = shard
    for k, owner in enumerate(ring_owners()):
        if k:
            held = ring_step(held)
        full = lax.dynamic_update_slice_in_dim(full, held, owner * size, 0)
        full = lax.dynamic_update_slice_in_dim(full, swap(held, "dp", 1), (owner ^ 1) * size, 0)
    return full


def ring_reduce(grad):
    size = grad.shape[1] // lax.axis_size("dp")
    owners = ring_owners()

    def columns(owner):
        return lax.dynamic_slice_in_dim(grad, owner * size, size, 1)

    other = swap(jnp.stack([columns(owner ^ 1) for owner in owners]), "dp", 1)

    def block(k):
        return columns(owners[k]).astype(F32) + other[k].astype(F32)

    total = block(1)
    for k in list(range(2, len(owners))) + [0]:
        total = block(k) + ring_step(total.astype(BF16)).astype(F32)
    return total


def core_halves(grad):
    count = lax.axis_size("dp")
    size = grad.shape[1] // count
    core = lax.axis_index("dp") % 2

    def half(which):
        return jnp.concatenate(
            [
                lax.dynamic_slice_in_dim(grad, (2 * z + which) * size, size, 1)
                for z in range(count // 2)
            ],
            axis=1,
        )

    other = half(1 - core)
    got = swap(other, "dp", 1)
    return (half(core).astype(F32) + got.astype(F32)).astype(BF16)


def after(value, *others):
    return lax.optimization_barrier((value,) + others)[0]


def ordered(ref, lead, offs_ref, runs):
    return jnp.concatenate(
        [
            ref[lead + (pl.ds(pl.multiple_of(offs_ref[i], 16), size), slice(None))]
            for i, size in runs
        ],
        axis=0,
    )


def put_ordered(ref, lead, offs_ref, runs, value):
    at = 0
    for i, size in runs:
        ref[lead + (pl.ds(pl.multiple_of(offs_ref[i], 16), size), slice(None))] = value[
            at : at + size
        ]
        at += size


CHUNK = 256
HEADS_STEP = LANES // HEAD_DIM


def lane_roll(value, shift):
    return pltpu.roll(value, shift % LANES, 1)


def masked(scores, start):
    own = scores[:, start:]
    rows = lax.broadcasted_iota(jnp.int32, own.shape, 0)
    cols = lax.broadcasted_iota(jnp.int32, own.shape, 1)
    own = jnp.where(rows >= cols, own, -jnp.inf)
    return jnp.concatenate([scores[:, :start], own], axis=1) if start else own


def attend_kernel(offs_ref, pre_ref, keep_ref, low_ref, high_ref, qkv_ref, ctx_ref, lse_ref, *, runs):
    for seq, seq_runs in enumerate(runs):
        attend_seq(
            offs_ref, pre_ref, keep_ref, low_ref, high_ref, qkv_ref, ctx_ref, lse_ref, seq, seq_runs
        )


def attend_seq(
    offs_ref, pre_ref, keep_ref, low_ref, high_ref, qkv_ref, ctx_ref, lse_ref, seq, runs
):
    half = ROT // 2
    scale = HEAD_DIM ** (-0.5)
    keep, low, high = keep_ref[...], low_ref[...], high_ref[...]
    for c in range(3):
        v = ordered(pre_ref, (c,), offs_ref, runs)
        if c < 2:
            v = v * keep + lane_roll(v, -half) * low + lane_roll(v, half) * high
        qkv_ref[c, seq] = v.astype(BF16)
    ctx_parts, lse_parts = [], []
    for start in range(0, SEQ_LEN, CHUNK):
        end = start + CHUNK
        ctxs, lses = [], []
        for h in range(HEADS_STEP):
            cols = slice(h * HEAD_DIM, (h + 1) * HEAD_DIM)
            q = qkv_ref[0, seq, start:end, cols]
            k = qkv_ref[1, seq, :end, cols]
            v = qkv_ref[2, seq, :end, cols]
            s = lax.dot_general(q * scale, k, NT, preferred_element_type=F32)
            s = masked(s, start)
            top = jnp.max(s, axis=-1, keepdims=True)
            e = jnp.exp(s - top)
            total = jnp.sum(e, axis=-1, keepdims=True)
            p = (e * (1.0 / total)).astype(BF16)
            ctxs.append(jnp.dot(p, v, preferred_element_type=F32).astype(BF16))
            lses.append(jnp.broadcast_to(top + jnp.log(total), (CHUNK, HEAD_DIM)))
        ctx_parts.append(jnp.concatenate(ctxs, axis=1))
        lse_parts.append(jnp.concatenate(lses, axis=1))
    put_ordered(ctx_ref, (), offs_ref, runs, jnp.concatenate(ctx_parts, axis=0))
    lse_ref[seq] = jnp.concatenate(lse_parts, axis=0)


def attend_back_kernel(offs_ref, *refs, runs):
    for seq, seq_runs in enumerate(runs):
        attend_back_seq(offs_ref, *refs, seq, seq_runs)


def attend_back_seq(
    offs_ref,
    qkv_ref,
    ctx_ref,
    gctx_ref,
    lse_ref,
    keep_ref,
    low_ref,
    high_ref,
    gpre_ref,
    bias_ref,
    seq,
    runs,
):
    half = ROT // 2
    scale = HEAD_DIM ** (-0.5)
    ctx = ordered(ctx_ref, (), offs_ref, runs)
    gctx = ordered(gctx_ref, (), offs_ref, runs)
    prod = gctx.astype(F32) * ctx.astype(F32)
    starts = list(range(0, SEQ_LEN, CHUNK))
    gq, gk, gv = [], [], []
    for h in range(HEADS_STEP):
        cols = slice(h * HEAD_DIM, (h + 1) * HEAD_DIM)
        dq_parts = []
        dk = [None] * len(starts)
        dv = [None] * len(starts)
        for i, start in enumerate(starts):
            end = start + CHUNK
            q = qkv_ref[0, seq, start:end, cols]
            k = qkv_ref[1, seq, :end, cols]
            v = qkv_ref[2, seq, :end, cols]
            g = gctx[start:end, cols]
            lse = lse_ref[seq, start:end, h * HEAD_DIM : h * HEAD_DIM + 1]
            delta = jnp.sum(prod[start:end, cols], axis=-1, keepdims=True)
            s = lax.dot_general(q * scale, k, NT, preferred_element_type=F32)
            p = jnp.exp(masked(s, start) - lse)
            dp = lax.dot_general(g, v, NT, preferred_element_type=F32)
            ds = (p * (dp - delta)).astype(BF16)
            p_low = p.astype(BF16)
            dq_parts.append(jnp.dot(ds, k, preferred_element_type=F32))
            dk_i = lax.dot_general(ds, q, TN, preferred_element_type=F32)
            dv_i = lax.dot_general(p_low, g, TN, preferred_element_type=F32)
            for j in range(i + 1):
                part = slice(j * CHUNK, (j + 1) * CHUNK)
                dk[j] = dk_i[part] if dk[j] is None else dk[j] + dk_i[part]
                dv[j] = dv_i[part] if dv[j] is None else dv[j] + dv_i[part]
        gq.append(jnp.concatenate(dq_parts, axis=0) * scale)
        gk.append(jnp.concatenate(dk, axis=0) * scale)
        gv.append(jnp.concatenate(dv, axis=0))
    keep, low, high = keep_ref[...], low_ref[...], high_ref[...]
    for c, parts in enumerate((gq, gk, gv)):
        v = jnp.concatenate(parts, axis=1)
        if c < 2:
            v = v * keep - lane_roll(v, -half) * low - lane_roll(v, half) * high
        v = v.astype(BF16)
        put_ordered(gpre_ref, (c,), offs_ref, runs, v)
        bias_ref[seq, c : c + 1] = jnp.sum(v.astype(F32), axis=0, keepdims=True)


def attend_specs(seqs, group_rows):
    table = pl.BlockSpec((SEQ_LEN, LANES), lambda h, f: (0, 0))
    framed3 = pl.BlockSpec((3, group_rows, LANES), lambda h, f: (0, 0, h))
    framed = pl.BlockSpec((group_rows, LANES), lambda h, f: (0, h))
    natural3 = pl.BlockSpec((3, seqs, SEQ_LEN, LANES), lambda h, f: (0, 0, 0, h))
    natural = pl.BlockSpec((seqs, SEQ_LEN, LANES), lambda h, f: (0, 0, h))
    bias = pl.BlockSpec((seqs, 3, LANES), lambda h, f: (0, 0, h))
    return table, framed3, framed, natural3, natural, bias


def sequence_runs(rows):
    pieces, per_seq = frame_pieces(rows)
    runs = [(i, hi - lo) for i, (_, lo, hi, _) in enumerate(pieces)]
    return tuple(tuple(runs[i : i + per_seq]) for i in range(0, len(runs), per_seq))


def attend(offs, pre, tables, runs):
    _, group_rows, cols = pre.shape
    seqs = group_rows // SEQ_LEN
    table, framed3, framed, natural3, natural, _ = attend_specs(seqs, group_rows)
    return pl.pallas_call(
        functools.partial(attend_kernel, runs=runs),
        out_shape=(
            jax.ShapeDtypeStruct((3, seqs, SEQ_LEN, cols), BF16),
            jax.ShapeDtypeStruct((group_rows, cols), BF16),
            jax.ShapeDtypeStruct((seqs, SEQ_LEN, cols), F32),
        ),
        grid_spec=pltpu.PrefetchScalarGridSpec(
            num_scalar_prefetch=1,
            grid=(cols // LANES,),
            in_specs=[framed3, table, table, table],
            out_specs=[natural3, framed, natural],
        ),
        name="attend",
    )(offs, pre, *tables)


def attend_back(offs, qkv, ctx, gctx, lse, tables, runs):
    _, seqs, _, cols = qkv.shape
    group_rows = seqs * SEQ_LEN
    table, framed3, framed, natural3, natural, bias = attend_specs(seqs, group_rows)
    return pl.pallas_call(
        functools.partial(attend_back_kernel, runs=runs),
        out_shape=(
            jax.ShapeDtypeStruct((3, group_rows, cols), BF16),
            jax.ShapeDtypeStruct((seqs, 3, cols), F32),
        ),
        grid_spec=pltpu.PrefetchScalarGridSpec(
            num_scalar_prefetch=1,
            grid=(cols // LANES,),
            in_specs=[natural3, framed, framed, natural, table, table, table],
            out_specs=[framed3, bias],
        ),
        name="attend_back",
    )(offs, qkv, ctx, gctx, lse, *tables)


def shards(
    layer_input,
    norm1_gain,
    norm1_bias,
    qkv_weight,
    qkv_bias,
    out_weight,
    norm2_gain,
    norm2_bias,
    gate_up_weight,
    down_weight,
    out_cotangent,
):
    rows, width = layer_input.shape
    part = norm1_gain.shape[0]
    dp_count = lax.axis_size("dp")
    dp_here = lax.axis_index("dp")
    head_cols = qkv_weight.shape[2]
    offs = frame_offsets(rows)
    runs = sequence_runs(rows)
    tables = rotary_lanes()

    qkv_local = lax.all_gather(qkv_weight, "dp", axis=1, tiled=True)
    gate_up_local = lax.all_gather(gate_up_weight, "dp", axis=1, tiled=True)
    down_local = lax.all_gather(down_weight, "dp", axis=1, tiled=True)

    packed = jnp.concatenate(
        [norm1_gain, norm1_bias, norm2_gain, norm2_bias, qkv_bias.reshape(-1)]
    )
    packed = lax.all_gather(packed, "dp", axis=0, tiled=False)
    x_rows = collect_rows(layer_input)
    cot_rows = collect_rows(after(out_cotangent, x_rows))
    gain_one, bias_one, gain_two, bias_two = (
        packed[:, k * part : (k + 1) * part].reshape(width).astype(F32) for k in range(4)
    )
    bias_local = (
        packed[:, 4 * part :].reshape(dp_count, 3, -1).transpose(1, 0, 2).reshape(3, head_cols)
    ).astype(F32)

    x_float = layer_input.astype(F32)
    hat_one, inv_one = layer_norm(x_float)
    out_turned = ring_gather(out_weight.T)
    rows_one = (layer_norm(x_rows.astype(F32))[0] * gain_one + bias_one).astype(BF16)
    pre = (
        jnp.einsum("rd,cdk->crk", rows_one, qkv_local, preferred_element_type=F32)
        + bias_local[:, None, :]
    )
    qkv_heads, context, lse = attend(offs, pre, tables, runs)
    parts = part_slices(rows)
    attn_terms = [
        lax.dot_general(context[at], out_turned, NT, preferred_element_type=F32).astype(BF16)
        for at in parts
    ]
    residual = x_float + spread_rows(attn_terms, rows)

    hat_two, inv_two = layer_norm(residual)
    rows_two = collect_rows((hat_two * gain_two + bias_two).astype(BF16))
    gate_proj = jnp.dot(rows_two, gate_up_local[0], preferred_element_type=F32)
    up_proj = jnp.dot(rows_two, gate_up_local[1], preferred_element_type=F32)
    sigmoid_gate = jax.nn.sigmoid(gate_proj)
    silu_gate = gate_proj * sigmoid_gate
    activation = (silu_gate * up_proj).astype(BF16)

    grad_down = lax.dot_general(
        activation, cot_rows, TN, preferred_element_type=F32
    ).astype(BF16)
    share_down = lax.psum_scatter(grad_down, "dp", scatter_dimension=1, tiled=True)
    share_down = share_down.astype(F32)
    grad_act = lax.dot_general(
        after(cot_rows, grad_down), down_local, NT, preferred_element_type=F32
    )
    grad_gate = (
        grad_act * up_proj * sigmoid_gate * (1.0 + gate_proj * (1.0 - sigmoid_gate))
    ).astype(BF16)
    grad_up = (grad_act * silu_gate).astype(BF16)
    back_terms = [
        (
            lax.dot_general(grad_gate[at], gate_up_local[0], NT, preferred_element_type=F32)
            + lax.dot_general(grad_up[at], gate_up_local[1], NT, preferred_element_type=F32)
        ).astype(BF16)
        for at in parts
    ]
    grad_normed_two = spread_rows(back_terms, rows)
    grad_gate_up = jnp.stack([grad_gate, grad_up])
    grad_wgate_up = jnp.einsum(
        "rd,crk->cdk",
        after(rows_two, *back_terms),
        grad_gate_up,
        preferred_element_type=F32,
    ).astype(BF16)
    share_gate_up = lax.psum_scatter(grad_wgate_up, "dp", scatter_dimension=1, tiled=True)
    share_gate_up = share_gate_up.astype(F32)
    grad_normed_two, _, mlp_act = lax.optimization_barrier(
        (grad_normed_two, grad_wgate_up, activation)
    )
    grad_resid = out_cotangent.astype(F32) + norm_back(
        grad_normed_two * gain_two, hat_two, inv_two
    )

    mlp_terms = jnp.dot(mlp_act, down_local, preferred_element_type=F32).astype(BF16)
    resid_rows, mlp_terms = lax.optimization_barrier(
        (collect_rows(grad_resid.astype(BF16)), mlp_terms)
    )
    grad_context = jnp.dot(resid_rows, out_turned, preferred_element_type=F32).astype(BF16)
    grad_pre, bias_sums = attend_back(offs, qkv_heads, context, grad_context, lse, tables, runs)
    grad_wqkv = jnp.einsum(
        "crk,rd->ckd", grad_pre, rows_one, preferred_element_type=F32
    ).astype(BF16)
    wqkv_half = core_halves(grad_wqkv.reshape(3 * head_cols, width))
    share_qkv = lax.psum_scatter(
        wqkv_half,
        "dp",
        scatter_dimension=1,
        tiled=True,
        axis_index_groups=[list(range(c, dp_count, 2)) for c in range(2)],
    )
    layer_output = (residual + spread_rows([mlp_terms[at] for at in parts], rows)).astype(BF16)
    late_pre = after(grad_pre, grad_wqkv)
    qkv_terms = [
        jnp.einsum(
            "crk,cdk->rd", late_pre[:, at], qkv_local, preferred_element_type=F32
        ).astype(BF16)
        for at in parts
    ]
    grad_normed_one = spread_rows(qkv_terms, rows)
    grad_wout = lax.dot_general(
        after(context, grad_wqkv), resid_rows, TN, preferred_element_type=F32
    ).astype(BF16)
    share_out = ring_reduce(grad_wout)
    grad_input = grad_resid + norm_back(grad_normed_one * gain_one, hat_one, inv_one)

    norm_sums = jnp.stack(
        [
            jnp.sum(grad_normed_one * hat_one, axis=0),
            jnp.sum(grad_normed_one, axis=0),
            jnp.sum(grad_normed_two * hat_two, axis=0),
            jnp.sum(grad_normed_two, axis=0),
        ]
    )
    norm_total, share_gate_up, share_down = lax.optimization_barrier(
        (total_over(norm_sums, "tensor"), share_gate_up, share_down)
    )
    norm_total = norm_total.reshape(-1)
    bias_total = jnp.sum(bias_sums, axis=0).reshape(-1)
    totals = total_over(jnp.concatenate([norm_total, bias_total]), "dp")
    share_qkv = after(share_qkv, totals)
    share_qkv = share_qkv.astype(F32).reshape(3, head_cols, part).transpose(0, 2, 1)
    norm_total = totals[: 4 * width].reshape(4, width)
    bias_total = totals[4 * width :].reshape(3, head_cols)
    share_norm = lax.dynamic_slice_in_dim(norm_total, dp_here * part, part, axis=1)
    bias_part = qkv_bias.shape[1]
    share_bias = lax.dynamic_slice_in_dim(bias_total, dp_here * bias_part, bias_part, axis=1)
    return (
        layer_output,
        grad_input,
        share_norm[0],
        share_norm[1],
        share_qkv,
        share_bias,
        share_out,
        share_norm[2],
        share_norm[3],
        share_gate_up,
        share_down,
    )


def solution(mesh):
    placed = (
        P(("dp", "tensor"), None),
        P("dp"),
        P("dp"),
        P(None, "dp", "tensor"),
        P(None, ("tensor", "dp")),
        P("tensor", "dp"),
        P("dp"),
        P("dp"),
        P(None, "dp", "tensor"),
        P("tensor", "dp"),
        P(("dp", "tensor"), None),
    )

    return jax.shard_map(
        shards,
        mesh=mesh,
        in_specs=placed,
        out_specs=(
            P(("dp", "tensor"), None),
            P(("dp", "tensor"), None),
            P("dp"),
            P("dp"),
            P(None, "dp", "tensor"),
            P(None, ("tensor", "dp")),
            P("tensor", "dp"),
            P("dp"),
            P("dp"),
            P(None, "dp", "tensor"),
            P("tensor", "dp"),
        ),
        check_vma=False,
    )
```

```python
import functools

import jax
import jax.numpy as jnp
from jax import lax
from jax.experimental import pallas as pl
from jax.experimental.pallas import tpu as pltpu
from jax.sharding import PartitionSpec as P


HEAD_DIM = 64
ROT = 16
SEQ_LEN = 512
LANES = 128
EPS = 1e-05
F32 = jnp.float32
BF16 = jnp.bfloat16
NT = (((1,), (1,)), ((), ()))
TN = (((0,), (0,)), ((), ()))


def layer_norm(values):
    row_mean = jnp.mean(values, axis=-1, keepdims=True)
    centered = values - row_mean
    inv_sigma = lax.rsqrt(jnp.mean(centered * centered, axis=-1, keepdims=True) + EPS)
    return (centered * inv_sigma, inv_sigma)


def norm_back(grad_hat, normed, inv_sigma):
    return inv_sigma * (
        grad_hat
        - jnp.mean(grad_hat, axis=-1, keepdims=True)
        - normed * jnp.mean(grad_hat * normed, axis=-1, keepdims=True)
    )


def rotary_lanes():
    half = ROT // 2
    frequency = 10000.0 ** (-(2.0 * jnp.arange(half, dtype=F32)) / ROT)
    angles = jnp.arange(SEQ_LEN, dtype=F32)[:, None] * frequency[None, :]
    cosine, sine = jnp.cos(angles), jnp.sin(angles)
    rest = HEAD_DIM - ROT
    zero = jnp.zeros((SEQ_LEN, half), F32)
    tail = jnp.zeros((SEQ_LEN, rest), F32)
    copies = LANES // HEAD_DIM
    keep = jnp.concatenate([cosine, cosine, tail + 1.0] * copies, axis=1)
    low = jnp.concatenate([-sine, zero, tail] * copies, axis=1)
    high = jnp.concatenate([zero, sine, tail] * copies, axis=1)
    return keep, low, high


def bits_of(axis):
    size = lax.axis_size(axis)
    return [1 << b for b in range(size.bit_length() - 1)]


def swap(value, axis, bit):
    return lax.ppermute(value, axis, [(i, i ^ bit) for i in range(lax.axis_size(axis))])


def total_over(value, axis):
    for bit in bits_of(axis):
        value = value + swap(value, axis, bit)
    return value


def row_parts(rows, count):
    tiles = rows // 16
    edges = [16 * (tiles * k // count) for k in range(count)] + [rows]
    return list(zip(edges[:-1], edges[1:]))


def part_plan(rows):
    bits = bits_of("tensor")
    return [
        (lo, hi, bits[k:] + bits[:k]) for k, (lo, hi) in enumerate(row_parts(rows, len(bits)))
    ]


def together(values):
    return list(lax.optimization_barrier(tuple(values)))


def collect_rows(block):
    plan = part_plan(block.shape[0])
    held = [block[lo:hi] for lo, hi, _ in plan]
    for j in range(len(plan)):
        got = []
        for h, (_, _, order) in zip(held, plan):
            got.append(swap(h, "tensor", order[j]))
        held = together(jnp.concatenate([h, g], axis=0) for h, g in zip(held, got))
    return jnp.concatenate(held, axis=0)


def part_slices(rows):
    count = lax.axis_size("tensor")
    return [slice(lo * count, hi * count) for lo, hi, _ in part_plan(rows)]


def spread_rows(terms, rows):
    plan = part_plan(rows)
    held = list(terms)
    for j in reversed(range(len(plan))):
        totals = []
        for h, (_, _, order) in zip(held, plan):
            half = h.shape[0] // 2
            got = swap(h[half:], "tensor", order[j])
            total = h[:half].astype(F32) + got.astype(F32)
            totals.append(total.astype(BF16) if j else total)
        held = together(totals)
    return jnp.concatenate(held, axis=0)


def frame_pieces(rows):
    count = lax.axis_size("tensor")
    per_seq = SEQ_LEN // rows
    return [
        (member, lo, hi, order)
        for member in range(count)
        for lo, hi, order in part_plan(rows)
    ], per_seq * len(part_plan(rows))


def frame_offsets(rows):
    count = lax.axis_size("tensor")
    here = lax.axis_index("tensor").astype(jnp.int32)
    places = []
    for member, lo, hi, order in frame_pieces(rows)[0]:
        other = here ^ member
        place = jnp.int32(0)
        for j, bit in enumerate(order):
            place = place + jnp.where((other & bit) != 0, 1 << j, 0)
        places.append(lo * count + place * (hi - lo))
    return jnp.stack(places).astype(jnp.int32)


def ring_step(value):
    count = lax.axis_size("dp")
    return lax.ppermute(value, "dp", [(i, (i + 2) % count) for i in range(count)])


def ring_owners():
    count = lax.axis_size("dp")
    here = lax.axis_index("dp")
    return [(here - 2 * k) % count for k in range(count // 2)]


def ring_gather(shard):
    count = lax.axis_size("dp")
    size = shard.shape[0]
    full = jnp.zeros((size * count,) + shard.shape[1:], shard.dtype)
    held = shard
    for k, owner in enumerate(ring_owners()):
        if k:
            held = ring_step(held)
        full = lax.dynamic_update_slice_in_dim(full, held, owner * size, 0)
        full = lax.dynamic_update_slice_in_dim(full, swap(held, "dp", 1), (owner ^ 1) * size, 0)
    return full


def ring_reduce(grad):
    size = grad.shape[1] // lax.axis_size("dp")
    owners = ring_owners()

    def columns(owner):
        return lax.dynamic_slice_in_dim(grad, owner * size, size, 1)

    other = swap(jnp.stack([columns(owner ^ 1) for owner in owners]), "dp", 1)

    def block(k):
        return columns(owners[k]).astype(F32) + other[k].astype(F32)

    total = block(1)
    for k in range(2, len(owners)):
        total = block(k) + ring_step(total.astype(BF16)).astype(F32)
    return block(0), ring_step(total.astype(BF16))


def core_halves(grad):
    count = lax.axis_size("dp")
    size = grad.shape[1] // count
    core = lax.axis_index("dp") % 2

    def half(which):
        return jnp.concatenate(
            [
                lax.dynamic_slice_in_dim(grad, (2 * z + which) * size, size, 1)
                for z in range(count // 2)
            ],
            axis=1,
        )

    other = half(1 - core)
    got = swap(other, "dp", 1)
    return (half(core).astype(F32) + got.astype(F32)).astype(BF16)


def after(value, *others):
    return lax.optimization_barrier((value,) + others)[0]


def ordered(ref, lead, offs_ref, runs):
    return jnp.concatenate(
        [
            ref[lead + (pl.ds(pl.multiple_of(offs_ref[i], 16), size), slice(None))]
            for i, size in runs
        ],
        axis=0,
    )


def put_ordered(ref, lead, offs_ref, runs, value):
    at = 0
    for i, size in runs:
        ref[lead + (pl.ds(pl.multiple_of(offs_ref[i], 16), size), slice(None))] = value[
            at : at + size
        ]
        at += size


CHUNK = 256
HEADS_STEP = LANES // HEAD_DIM


def lane_roll(value, shift):
    return pltpu.roll(value, shift % LANES, 1)


def masked(scores, start):
    own = scores[:, start:]
    rows = lax.broadcasted_iota(jnp.int32, own.shape, 0)
    cols = lax.broadcasted_iota(jnp.int32, own.shape, 1)
    own = jnp.where(rows >= cols, own, -jnp.inf)
    return jnp.concatenate([scores[:, :start], own], axis=1) if start else own


def attend_kernel(offs_ref, pre_ref, keep_ref, low_ref, high_ref, qkv_ref, ctx_ref, lse_ref, *, runs):
    for seq, seq_runs in enumerate(runs):
        attend_seq(
            offs_ref, pre_ref, keep_ref, low_ref, high_ref, qkv_ref, ctx_ref, lse_ref, seq, seq_runs
        )


def attend_seq(
    offs_ref, pre_ref, keep_ref, low_ref, high_ref, qkv_ref, ctx_ref, lse_ref, seq, runs
):
    half = ROT // 2
    scale = HEAD_DIM ** (-0.5)
    keep, low, high = keep_ref[...], low_ref[...], high_ref[...]
    for c in range(3):
        v = ordered(pre_ref, (c,), offs_ref, runs)
        if c < 2:
            v = v * keep + lane_roll(v, -half) * low + lane_roll(v, half) * high
        qkv_ref[c, seq] = v.astype(BF16)
    ctx_parts, lse_parts = [], []
    for start in range(0, SEQ_LEN, CHUNK):
        end = start + CHUNK
        ctxs, lses = [], []
        for h in range(HEADS_STEP):
            cols = slice(h * HEAD_DIM, (h + 1) * HEAD_DIM)
            q = qkv_ref[0, seq, start:end, cols]
            k = qkv_ref[1, seq, :end, cols]
            v = qkv_ref[2, seq, :end, cols]
            s = lax.dot_general(q * scale, k, NT, preferred_element_type=F32)
            s = masked(s, start)
            top = jnp.max(s, axis=-1, keepdims=True)
            e = jnp.exp(s - top)
            total = jnp.sum(e, axis=-1, keepdims=True)
            p = (e * (1.0 / total)).astype(BF16)
            ctxs.append(jnp.dot(p, v, preferred_element_type=F32).astype(BF16))
            lses.append(jnp.broadcast_to(top + jnp.log(total), (CHUNK, HEAD_DIM)))
        ctx_parts.append(jnp.concatenate(ctxs, axis=1))
        lse_parts.append(jnp.concatenate(lses, axis=1))
    put_ordered(ctx_ref, (), offs_ref, runs, jnp.concatenate(ctx_parts, axis=0))
    lse_ref[seq] = jnp.concatenate(lse_parts, axis=0)


def attend_back_kernel(offs_ref, *refs, runs):
    for seq, seq_runs in enumerate(runs):
        attend_back_seq(offs_ref, *refs, seq, seq_runs)


def attend_back_seq(
    offs_ref,
    qkv_ref,
    ctx_ref,
    gctx_ref,
    lse_ref,
    keep_ref,
    low_ref,
    high_ref,
    gpre_ref,
    bias_ref,
    seq,
    runs,
):
    half = ROT // 2
    scale = HEAD_DIM ** (-0.5)
    ctx = ordered(ctx_ref, (), offs_ref, runs)
    gctx = ordered(gctx_ref, (), offs_ref, runs)
    prod = gctx.astype(F32) * ctx.astype(F32)
    starts = list(range(0, SEQ_LEN, CHUNK))
    gq, gk, gv = [], [], []
    for h in range(HEADS_STEP):
        cols = slice(h * HEAD_DIM, (h + 1) * HEAD_DIM)
        dq_parts = []
        dk = [None] * len(starts)
        dv = [None] * len(starts)
        for i, start in enumerate(starts):
            end = start + CHUNK
            q = qkv_ref[0, seq, start:end, cols]
            k = qkv_ref[1, seq, :end, cols]
            v = qkv_ref[2, seq, :end, cols]
            g = gctx[start:end, cols]
            lse = lse_ref[seq, start:end, h * HEAD_DIM : h * HEAD_DIM + 1]
            delta = jnp.sum(prod[start:end, cols], axis=-1, keepdims=True)
            s = lax.dot_general(q * scale, k, NT, preferred_element_type=F32)
            p = jnp.exp(masked(s, start) - lse)
            dp = lax.dot_general(g, v, NT, preferred_element_type=F32)
            ds = (p * (dp - delta)).astype(BF16)
            p_low = p.astype(BF16)
            dq_parts.append(jnp.dot(ds, k, preferred_element_type=F32))
            dk_i = lax.dot_general(ds, q, TN, preferred_element_type=F32)
            dv_i = lax.dot_general(p_low, g, TN, preferred_element_type=F32)
            for j in range(i + 1):
                part = slice(j * CHUNK, (j + 1) * CHUNK)
                dk[j] = dk_i[part] if dk[j] is None else dk[j] + dk_i[part]
                dv[j] = dv_i[part] if dv[j] is None else dv[j] + dv_i[part]
        gq.append(jnp.concatenate(dq_parts, axis=0) * scale)
        gk.append(jnp.concatenate(dk, axis=0) * scale)
        gv.append(jnp.concatenate(dv, axis=0))
    keep, low, high = keep_ref[...], low_ref[...], high_ref[...]
    for c, parts in enumerate((gq, gk, gv)):
        v = jnp.concatenate(parts, axis=1)
        if c < 2:
            v = v * keep - lane_roll(v, -half) * low - lane_roll(v, half) * high
        v = v.astype(BF16)
        put_ordered(gpre_ref, (c,), offs_ref, runs, v)
        bias_ref[seq, c : c + 1] = jnp.sum(v.astype(F32), axis=0, keepdims=True)


def attend_specs(seqs, group_rows):
    table = pl.BlockSpec((SEQ_LEN, LANES), lambda h, f: (0, 0))
    framed3 = pl.BlockSpec((3, group_rows, LANES), lambda h, f: (0, 0, h))
    framed = pl.BlockSpec((group_rows, LANES), lambda h, f: (0, h))
    natural3 = pl.BlockSpec((3, seqs, SEQ_LEN, LANES), lambda h, f: (0, 0, 0, h))
    natural = pl.BlockSpec((seqs, SEQ_LEN, LANES), lambda h, f: (0, 0, h))
    bias = pl.BlockSpec((seqs, 3, LANES), lambda h, f: (0, 0, h))
    return table, framed3, framed, natural3, natural, bias


def sequence_runs(rows):
    pieces, per_seq = frame_pieces(rows)
    runs = [(i, hi - lo) for i, (_, lo, hi, _) in enumerate(pieces)]
    return tuple(tuple(runs[i : i + per_seq]) for i in range(0, len(runs), per_seq))


def attend(offs, pre, tables, runs):
    _, group_rows, cols = pre.shape
    seqs = group_rows // SEQ_LEN
    table, framed3, framed, natural3, natural, _ = attend_specs(seqs, group_rows)
    return pl.pallas_call(
        functools.partial(attend_kernel, runs=runs),
        out_shape=(
            jax.ShapeDtypeStruct((3, seqs, SEQ_LEN, cols), BF16),
            jax.ShapeDtypeStruct((group_rows, cols), BF16),
            jax.ShapeDtypeStruct((seqs, SEQ_LEN, cols), F32),
        ),
        grid_spec=pltpu.PrefetchScalarGridSpec(
            num_scalar_prefetch=1,
            grid=(cols // LANES,),
            in_specs=[framed3, table, table, table],
            out_specs=[natural3, framed, natural],
        ),
        name="attend",
    )(offs, pre, *tables)


def attend_back(offs, qkv, ctx, gctx, lse, tables, runs):
    _, seqs, _, cols = qkv.shape
    group_rows = seqs * SEQ_LEN
    table, framed3, framed, natural3, natural, bias = attend_specs(seqs, group_rows)
    return pl.pallas_call(
        functools.partial(attend_back_kernel, runs=runs),
        out_shape=(
            jax.ShapeDtypeStruct((3, group_rows, cols), BF16),
            jax.ShapeDtypeStruct((seqs, 3, cols), F32),
        ),
        grid_spec=pltpu.PrefetchScalarGridSpec(
            num_scalar_prefetch=1,
            grid=(cols // LANES,),
            in_specs=[natural3, framed, framed, natural, table, table, table],
            out_specs=[framed3, bias],
        ),
        name="attend_back",
    )(offs, qkv, ctx, gctx, lse, *tables)


def shards(
    layer_input,
    norm1_gain,
    norm1_bias,
    qkv_weight,
    qkv_bias,
    out_weight,
    norm2_gain,
    norm2_bias,
    gate_up_weight,
    down_weight,
    out_cotangent,
):
    rows, width = layer_input.shape
    part = norm1_gain.shape[0]
    dp_count = lax.axis_size("dp")
    dp_here = lax.axis_index("dp")
    head_cols = qkv_weight.shape[2]
    offs = frame_offsets(rows)
    runs = sequence_runs(rows)
    tables = rotary_lanes()

    qkv_local = lax.all_gather(qkv_weight, "dp", axis=1, tiled=True)
    gate_up_local = lax.all_gather(gate_up_weight, "dp", axis=1, tiled=True)
    down_local = lax.all_gather(down_weight, "dp", axis=1, tiled=True)

    packed = jnp.concatenate(
        [norm1_gain, norm1_bias, norm2_gain, norm2_bias, qkv_bias.reshape(-1)]
    )
    packed = lax.all_gather(packed, "dp", axis=0, tiled=False)
    x_rows = collect_rows(layer_input)
    cot_rows = collect_rows(after(out_cotangent, x_rows))
    gain_one, bias_one, gain_two, bias_two = (
        packed[:, k * part : (k + 1) * part].reshape(width).astype(F32) for k in range(4)
    )
    bias_local = (
        packed[:, 4 * part :].reshape(dp_count, 3, -1).transpose(1, 0, 2).reshape(3, head_cols)
    ).astype(F32)

    x_float = layer_input.astype(F32)
    hat_one, inv_one = layer_norm(x_float)
    out_turned = ring_gather(out_weight.T)
    rows_one = (layer_norm(x_rows.astype(F32))[0] * gain_one + bias_one).astype(BF16)
    pre = (
        jnp.einsum("rd,cdk->crk", rows_one, qkv_local, preferred_element_type=F32)
        + bias_local[:, None, :]
    )
    qkv_heads, context, lse = attend(offs, pre, tables, runs)
    parts = part_slices(rows)
    attn_terms = [
        lax.dot_general(context[at], out_turned, NT, preferred_element_type=F32).astype(BF16)
        for at in parts
    ]
    residual = x_float + spread_rows(attn_terms, rows)

    hat_two, inv_two = layer_norm(residual)
    rows_two = collect_rows((hat_two * gain_two + bias_two).astype(BF16))
    gate_proj = jnp.dot(rows_two, gate_up_local[0], preferred_element_type=F32)
    up_proj = jnp.dot(rows_two, gate_up_local[1], preferred_element_type=F32)
    sigmoid_gate = jax.nn.sigmoid(gate_proj)
    silu_gate = gate_proj * sigmoid_gate
    activation = (silu_gate * up_proj).astype(BF16)

    grad_down = lax.dot_general(
        activation, cot_rows, TN, preferred_element_type=F32
    ).astype(BF16)
    share_down = lax.psum_scatter(grad_down, "dp", scatter_dimension=1, tiled=True)
    share_down = share_down.astype(F32)
    grad_act = lax.dot_general(
        after(cot_rows, grad_down), down_local, NT, preferred_element_type=F32
    )
    grad_gate = (
        grad_act * up_proj * sigmoid_gate * (1.0 + gate_proj * (1.0 - sigmoid_gate))
    ).astype(BF16)
    grad_up = (grad_act * silu_gate).astype(BF16)
    back_terms = [
        (
            lax.dot_general(grad_gate[at], gate_up_local[0], NT, preferred_element_type=F32)
            + lax.dot_general(grad_up[at], gate_up_local[1], NT, preferred_element_type=F32)
        ).astype(BF16)
        for at in parts
    ]
    grad_normed_two = spread_rows(back_terms, rows)
    grad_gate_up = jnp.stack([grad_gate, grad_up])
    grad_wgate_up = jnp.einsum(
        "rd,crk->cdk",
        after(rows_two, *back_terms),
        grad_gate_up,
        preferred_element_type=F32,
    ).astype(BF16)
    share_gate_up = lax.psum_scatter(grad_wgate_up, "dp", scatter_dimension=1, tiled=True)
    share_gate_up = share_gate_up.astype(F32)
    grad_normed_two, _, mlp_act = lax.optimization_barrier(
        (grad_normed_two, grad_wgate_up, activation)
    )
    grad_resid = out_cotangent.astype(F32) + norm_back(
        grad_normed_two * gain_two, hat_two, inv_two
    )

    mlp_terms = jnp.dot(mlp_act, down_local, preferred_element_type=F32).astype(BF16)
    resid_rows, mlp_terms = lax.optimization_barrier(
        (collect_rows(grad_resid.astype(BF16)), mlp_terms)
    )
    grad_context = jnp.dot(resid_rows, out_turned, preferred_element_type=F32).astype(BF16)
    grad_pre, bias_sums = attend_back(offs, qkv_heads, context, grad_context, lse, tables, runs)
    grad_wqkv = jnp.einsum(
        "crk,rd->ckd", grad_pre, rows_one, preferred_element_type=F32
    ).astype(BF16)
    wqkv_half = core_halves(grad_wqkv.reshape(3 * head_cols, width))
    share_qkv = lax.psum_scatter(
        wqkv_half,
        "dp",
        scatter_dimension=1,
        tiled=True,
        axis_index_groups=[list(range(c, dp_count, 2)) for c in range(2)],
    )
    layer_output = (residual + spread_rows([mlp_terms[at] for at in parts], rows)).astype(BF16)
    late_pre = after(grad_pre, grad_wqkv)
    qkv_terms = [
        jnp.einsum(
            "crk,cdk->rd", late_pre[:, at], qkv_local, preferred_element_type=F32
        ).astype(BF16)
        for at in parts
    ]
    grad_normed_one = spread_rows(qkv_terms, rows)
    grad_wout = lax.dot_general(
        after(context, grad_wqkv), resid_rows, TN, preferred_element_type=F32
    ).astype(BF16)
    own_out, got_out = ring_reduce(grad_wout)
    grad_input = grad_resid + norm_back(grad_normed_one * gain_one, hat_one, inv_one)

    norm_sums = jnp.stack(
        [
            jnp.sum(grad_normed_one * hat_one, axis=0),
            jnp.sum(grad_normed_one, axis=0),
            jnp.sum(grad_normed_two * hat_two, axis=0),
            jnp.sum(grad_normed_two, axis=0),
        ]
    )
    norm_total, share_gate_up, share_down = lax.optimization_barrier(
        (total_over(norm_sums, "tensor"), share_gate_up, share_down)
    )
    norm_total = norm_total.reshape(-1)
    bias_total = jnp.sum(bias_sums, axis=0).reshape(-1)
    totals = total_over(jnp.concatenate([norm_total, bias_total]), "dp")
    share_qkv = after(share_qkv, totals)
    share_out = own_out + after(got_out, totals).astype(F32)
    share_qkv = share_qkv.astype(F32).reshape(3, head_cols, part).transpose(0, 2, 1)
    norm_total = totals[: 4 * width].reshape(4, width)
    bias_total = totals[4 * width :].reshape(3, head_cols)
    share_norm = lax.dynamic_slice_in_dim(norm_total, dp_here * part, part, axis=1)
    bias_part = qkv_bias.shape[1]
    share_bias = lax.dynamic_slice_in_dim(bias_total, dp_here * bias_part, bias_part, axis=1)
    return (
        layer_output,
        grad_input,
        share_norm[0],
        share_norm[1],
        share_qkv,
        share_bias,
        share_out,
        share_norm[2],
        share_norm[3],
        share_gate_up,
        share_down,
    )


def solution(mesh):
    placed = (
        P(("dp", "tensor"), None),
        P("dp"),
        P("dp"),
        P(None, "dp", "tensor"),
        P(None, ("tensor", "dp")),
        P("tensor", "dp"),
        P("dp"),
        P("dp"),
        P(None, "dp", "tensor"),
        P("tensor", "dp"),
        P(("dp", "tensor"), None),
    )

    return jax.shard_map(
        shards,
        mesh=mesh,
        in_specs=placed,
        out_specs=(
            P(("dp", "tensor"), None),
            P(("dp", "tensor"), None),
            P("dp"),
            P("dp"),
            P(None, "dp", "tensor"),
            P(None, ("tensor", "dp")),
            P("tensor", "dp"),
            P("dp"),
            P("dp"),
            P(None, "dp", "tensor"),
            P("tensor", "dp"),
        ),
        check_vma=False,
    )
```
